256 devices in a mesh: dp: 4 (over y_hi, core), expert: 64 (over x, z, y_lo).
Axes of the slice: x: 4, y: 4 (y_hi: 2, y_lo: 2; y = y_hi * 2 + y_lo), z: 8, core: 2. Of those that a mesh axis runs over, the one named last changes fastest.
Arguments:
- tokens: bfloat16 [4, 8192, 3584], P('dp', 'expert'), may hold values from -6 to 6
- cotangent: bfloat16 [4, 8192, 1024], P('dp', 'expert'), may hold values from -12 to 12
- gate_weights: float32 [4, 8192], replicated, may hold values from 0.1 to 1
- tile_expert: int32 [4, 64], replicated, may hold values from 0 to 63, as said below
- w_gate: bfloat16 [64, 3584, 1024], P('expert', None, 'dp'), may hold values from -0.09375 to 0.09375
- w_up: bfloat16 [64, 3584, 1024], P('expert', None, 'dp'), may hold values from -0.09375 to 0.09375
Outputs:
- d_tokens: bfloat16 [4, 8192, 3584], P('dp', 'expert')
- hidden: bfloat16 [4, 8192, 1024], P(None, 'expert', 'dp')
- grad_gate: bfloat16 [64, 3584, 1024], P('expert', None, 'dp')
- grad_up: bfloat16 [64, 3584, 1024], P('expert', None, 'dp')
The draws below stay inside these ranges and needn't reach their ends.
Inputs may be any that keep to these rules, and one draw needn't show every extreme that they name: tile_expert[g, j] is either j or (j + 1) mod 64: the expert of the tile's own index of the expert axis or of the next index round the closed cycle.
All inputs are finite; a program needn't handle non-finite values.
Results may differ from the reference program's by a relative error of at most 0.009.
Values may be sent and summed in bfloat16 or wider, within the bound.
A program may use at most 128 MiB of HBM per device.

```python
import jax
import jax.numpy as jnp
from jax import lax

D = 3584
HID = 1024
TILE = 128
TILES_DEV = 1
GROUPS = 4
EXPERTS = 64
CYCLE_ROWS = 8192
CYCLE_TILES = 64


def draw_tile_expert(key, part):
    offsets = jax.random.randint(jax.random.fold_in(key, 11), (GROUPS, CYCLE_TILES), 0, 2)
    places = jnp.arange(CYCLE_TILES, dtype=jnp.int32) // TILES_DEV
    return ((places[None, :] + offsets) % EXPERTS).astype(jnp.int32)


def block_levels(rng, shape, shards, least, largest):
    def one(position, shards_of):
        draws = jax.random.uniform(jax.random.fold_in(jax.random.fold_in(rng, 6), position), (shards_of,), jnp.float32, least / len(shards), largest / len(shards))
        return jnp.repeat(jnp.exp(draws), shape[position] // shards_of).reshape((-1,) + (1,) * (len(shape) - position - 1))

    loudness = one(*shards[0])
    for cut in shards[1:]:
        loudness = loudness * one(*cut)
    return loudness


def gaussian(rng, shape, deviation, most, split=(), kind=jnp.bfloat16):
    loudness = block_levels(rng, shape, split, -0.22, 0.18) if split else 1.0
    drawn = jax.random.normal(rng, shape, jnp.float32) * deviation * loudness
    return jnp.minimum(jnp.maximum(drawn, -most), most).astype(kind)


def setup_inputs(seed: int = 0) -> dict:
    arg_keys = jax.random.split(jax.random.key(seed), 7)
    return {
        "tokens": gaussian(arg_keys[0], (GROUPS, CYCLE_ROWS, D), 1.0, 6.0, ((0, 4), (1, 64))),
        "cotangent": gaussian(arg_keys[1], (GROUPS, CYCLE_ROWS, HID), 2.0, 12.0, ((0, 4), (1, 64))),
        "gate_weights": jnp.clip(jax.random.uniform(arg_keys[2], (GROUPS, CYCLE_ROWS), jnp.float32, 0.1, 1.0), 0.1, 1.0),
        "tile_expert": draw_tile_expert(jax.random.fold_in(arg_keys[6], 71), 0),
        "w_gate": gaussian(arg_keys[4], (EXPERTS, D, HID), D ** -0.5, 0.09375, ((0, 64), (2, 4))),
        "w_up": gaussian(arg_keys[5], (EXPERTS, D, HID), D ** -0.5, 0.09375, ((0, 64), (2, 4))),
    }


def reference(tokens, cotangent, gate_weights, tile_expert, w_gate, w_up):
    groups = tokens.shape[0]
    cycle_count = w_gate.shape[0]
    row_count = tokens.shape[1] // cycle_count
    tile_count = row_count // TILE
    model_width = tokens.shape[2]
    quarter = HID // groups
    tile_rows = tokens.reshape(groups, cycle_count, row_count, model_width)
    tile_grads = cotangent.reshape(groups, cycle_count, row_count, HID)
    row_weights = gate_weights.reshape(groups, cycle_count, row_count)
    owners = jnp.repeat(tile_expert.reshape(groups, cycle_count, tile_count), TILE, axis=2, total_repeat_length=row_count)

    def select_at(source, slot_index):
        return lax.dynamic_index_in_dim(source, slot_index, 1, keepdims=False)

    def per_expert(expert):
        previous = (expert + cycle_count - 1) % cycle_count
        cand_rows = jnp.concatenate([select_at(tile_rows, expert), select_at(tile_rows, previous)], 1)
        cand_grads = jnp.concatenate([select_at(tile_grads, expert), select_at(tile_grads, previous)], 1)
        cand_weights = jnp.concatenate([select_at(row_weights, expert), select_at(row_weights, previous)], 1)
        cand_owners = jnp.concatenate([select_at(owners, expert), select_at(owners, previous)], 1)
        row_scale = jnp.where(cand_owners == expert, cand_weights, jnp.zeros_like(cand_weights)).reshape(-1, 1)
        flat_rows = cand_rows.reshape(-1, model_width)
        gate_panel = lax.dynamic_index_in_dim(w_gate, expert, 0, keepdims=False)
        up_panel = lax.dynamic_index_in_dim(w_up, expert, 0, keepdims=False)
        gate_val = jnp.dot(flat_rows, gate_panel, preferred_element_type=jnp.float32)
        up_val = jnp.dot(flat_rows, up_panel, preferred_element_type=jnp.float32)
        sigmoid_val = jax.nn.sigmoid(gate_val)
        activation = gate_val * sigmoid_val
        hidden_rows = (row_scale * activation * up_val).astype(jnp.bfloat16)
        act_grad = row_scale * cand_grads.reshape(-1, HID).astype(jnp.float32)
        up_grad = (act_grad * activation).astype(jnp.bfloat16)
        gate_grad = (act_grad * up_val * sigmoid_val * (1.0 + gate_val * (1.0 - sigmoid_val))).astype(jnp.bfloat16)
        row_total = jnp.zeros((flat_rows.shape[0], model_width), jnp.float32)
        for quarter_index in range(groups):
            start_col = quarter_index * quarter
            part_sum = jnp.dot(gate_grad[:, start_col:start_col + quarter], gate_panel[:, start_col:start_col + quarter].T, preferred_element_type=jnp.float32)
            part_sum = part_sum + jnp.dot(up_grad[:, start_col:start_col + quarter], up_panel[:, start_col:start_col + quarter].T, preferred_element_type=jnp.float32)
            rounded = lax.optimization_barrier(part_sum.astype(jnp.bfloat16))
            row_total = row_total + rounded.astype(jnp.float32)
        row_total = row_total.astype(jnp.bfloat16).reshape(groups, 2 * row_count, model_width)
        hidden_rows = hidden_rows.reshape(groups, 2 * row_count, HID)
        grad_gate = (jnp.dot(flat_rows.T, gate_grad, preferred_element_type=jnp.float32) / TILE).astype(jnp.bfloat16)
        grad_up = (jnp.dot(flat_rows.T, up_grad, preferred_element_type=jnp.float32) / TILE).astype(jnp.bfloat16)
        return (row_total[:, :row_count], row_total[:, row_count:], hidden_rows[:, :row_count], hidden_rows[:, row_count:], grad_gate, grad_up)

    own_rows, prev_rows, own_hidden, prev_hidden, grad_gate, grad_up = lax.map(per_expert, jnp.arange(cycle_count, dtype=jnp.int32))

    def combine(own_part, prev_part):
        joined = own_part.astype(jnp.float32) + jnp.roll(prev_part, -1, axis=0).astype(jnp.float32)
        joined = joined.astype(jnp.bfloat16)
        return jnp.transpose(joined, (1, 0, 2, 3)).reshape(groups, cycle_count * row_count, joined.shape[-1])

    return combine(own_rows, prev_rows), combine(own_hidden, prev_hidden), grad_gate, grad_up
```

```python
import functools

import jax
import jax.numpy as jnp
from jax import lax
from jax.experimental import pallas as pl
from jax.experimental.pallas import tpu as pltpu
from jax.sharding import PartitionSpec as P

MESH = pl.DeviceIdType.MESH
F32 = jnp.float32
BF16 = jnp.bfloat16
K = 4
N_COLS = 512


def dot_nn(a, b):
    return lax.dot_general(a, b, (((1,), (0,)), ((), ())), preferred_element_type=F32)


def dot_nt(a, b):
    return lax.dot_general(a, b, (((1,), (1,)), ((), ())), preferred_element_type=F32)


def dot_tn(a, b):
    return lax.dot_general(a, b, (((0,), (0,)), ((), ())), preferred_element_type=F32)


def kernel(
    experts,
    tok, cot, gw, te, wg_hbm, wu_hbm,
    dtok, hid, ggrad, ugrad,
    xr, ch, cs, gwv, wg, wu, gu, hv, hb, po, ps, sp, mv, zc, fin, wgo, wuo,
    s_ring, r_ring, s_opp, r_opp, s_z, r_z, s_sib, r_sib,
    s_cot, r_cot, s_ps, r_ps, s_m, r_m, s_zc, r_zc, s_fin, r_fin, s_hid, r_hid,
    l_in, l_gw, l_hid, l_wg, l_dt,
):
    tile = tok.shape[1]
    width = tok.shape[2]
    quarter = wg_hbm.shape[2]
    half = 2 * quarter
    rows = tile // K
    d = lax.axis_index("dp")
    e = lax.axis_index("expert")
    hi, c = d // 2, d % 2
    lo = e % 2
    prev = (e + experts - 1) % experts

    y_e = e + 1 - 2 * lo
    yp = ((d + 2 * lo) % 4, y_e)
    ym = ((d + 2 * (1 - lo)) % 4, y_e)
    sib = (d + 1 - 2 * c, e)
    zn = (d, (e + 2) % experts)
    zp = (d, (e + experts - 2) % experts)
    nxt = (d, (e + 1) % experts)
    prv = (d, prev)

    def remote(src, dst, send, recv, dev):
        return pltpu.make_async_remote_copy(
            src_ref=src, dst_ref=dst, send_sem=send, recv_sem=recv, device_id=dev, device_id_type=MESH
        )

    def arrived(dst, recv):
        remote(dst, dst, s_m.at[0], recv, sib).wait_recv()

    def sent(src, send):
        remote(src, src, send, r_m.at[0], sib).wait_send()

    def chunk(k, base=0, count=1):
        return pl.ds(base + k * rows, rows * count)

    even = lo == 0
    odd = lo == 1

    own_x = pltpu.make_async_copy(tok.at[0], xr.at[0, pl.ds(0, tile)], l_in.at[0])
    own_c = pltpu.make_async_copy(
        cot.at[0, :, pl.ds(pl.multiple_of(hi * half, half), half)], ch.at[0], l_in.at[1]
    )
    load_g = pltpu.make_async_copy(wg_hbm.at[0], wg, l_in.at[2])
    load_u = pltpu.make_async_copy(wu_hbm.at[0], wu, l_in.at[3])
    gw_own = pltpu.make_async_copy(gw.at[:, pl.ds(pl.multiple_of(e * tile, tile), tile)], gwv.at[0], l_gw.at[0])
    gw_prev = pltpu.make_async_copy(
        gw.at[:, pl.ds(pl.multiple_of(prev * tile, tile), tile)], gwv.at[1], l_gw.at[1]
    )
    own_x.start()
    own_c.start()
    load_g.start()
    load_u.start()
    gw_own.start()
    gw_prev.start()

    barrier = pltpu.get_barrier_semaphore()
    for dev in (yp, ym, sib):
        pl.semaphore_signal(barrier, inc=1, device_id=dev, device_id_type=MESH)

    @pl.when(even)
    def _():
        pl.semaphore_signal(barrier, inc=1, device_id=zn, device_id_type=MESH)
        pl.semaphore_signal(barrier, inc=1, device_id=zp, device_id_type=MESH)
        pl.semaphore_wait(barrier, 6)

    @pl.when(odd)
    def _():
        pl.semaphore_signal(barrier, inc=1, device_id=nxt, device_id_type=MESH)
        pl.semaphore_wait(barrier, 3)

    to1 = (1 + 3 * lo, 0)
    to3 = (3 + lo, tile * lo)
    at1 = (4 - 3 * lo, 0)
    at3 = (4 - lo, tile * (1 - lo))

    def ring1(k, src, slot, base):
        return remote(src, xr.at[slot, chunk(k, base)], s_ring.at[k], r_ring.at[k], yp)

    def ring3(k, src, slot, base):
        return remote(src, xr.at[slot, chunk(k, base)], s_ring.at[K + k], r_ring.at[K + k], ym)

    h_yp = lax.rem(hi + lo, 2)
    h_ym = lax.rem(hi + 1 - lo, 2)
    cot1 = remote(
        cot.at[0, :, pl.ds(pl.multiple_of(h_yp * half, half), half)], ch.at[1 + 3 * lo], s_cot.at[0], r_cot.at[0], yp
    )
    cot3 = remote(
        cot.at[0, :, pl.ds(pl.multiple_of(h_ym * half, half), half)], ch.at[3 + 2 * lo], s_cot.at[1], r_cot.at[1], ym
    )

    for k in range(K):
        ring1(k, tok.at[0, chunk(k)], *to1).start()
        ring3(K - 1 - k, tok.at[0, chunk(K - 1 - k)], *to3).start()
        if k == 0:
            cot1.start()
            cot3.start()

    mine = pl.ds(pl.multiple_of(c * quarter, quarter), quarter)
    other = pl.ds(pl.multiple_of((1 - c) * quarter, quarter), quarter)

    def sib_x(s):
        return remote(xr.at[s, pl.ds(0, tile)], xr.at[s, pl.ds(tile, tile)], s_sib.at[s], r_sib.at[s], sib)

    def sib_c(s):
        return remote(ch.at[s, :, other], cs.at[s], s_cot.at[5 + s], r_cot.at[5 + s], sib)

    def to_sibling(s):
        sib_x(s).start()
        sib_c(s).start()

    def from_sibling(s):
        sib_x(s).wait_recv()
        sib_c(s).wait_recv()

    own_x.wait()
    own_c.wait()
    to_sibling(0)

    eye = lax.broadcasted_iota(jnp.int32, (tile, tile), 0) == lax.broadcasted_iota(jnp.int32, (tile, tile), 1)
    gw_own.wait()
    gw_prev.wait()

    def scale_of(group, place, which):
        line = gwv[which, pl.ds(group, 1), :]
        routed = jnp.where(te[group, place] == e, jnp.float32(1.0), jnp.float32(0.0))
        spread = jnp.where(eye, jnp.broadcast_to(line, (tile, tile)), jnp.float32(0.0))
        return jnp.sum(spread, axis=1, keepdims=True) * routed

    def group_half(s):
        return (hi, (hi + 1 - lo) % 2, 1 - hi, (hi + lo) % 2)[s]

    def forward(s, dyn):
        gh, place, which = s
        x = xr[dyn]
        gate = dot_nn(x, wg[...])
        up = dot_nn(x, wu[...])
        for part in range(2):
            group = gh * 2 + (c if part == 0 else 1 - c)
            w = scale_of(group, place, which)
            r = slice(part * tile, (part + 1) * tile)
            dh = (ch[dyn, :, mine] if part == 0 else cs[dyn]).astype(F32)
            g, u = gate[r], up[r]
            sg = jax.nn.sigmoid(g)
            act = g * sg
            hv[dyn, r, :] = ((w * act) * u).astype(BF16)
            ag = w * dh
            gu[dyn, r, 0:quarter] = (ag * u * sg * (1.0 + g * (1.0 - sg))).astype(BF16)
            gu[dyn, r, quarter:half] = (ag * act).astype(BF16)

    def input_grad(dyn):
        gg = gu[dyn, :, 0:quarter]
        ug = gu[dyn, :, quarter:half]

        @pl.loop(0, width // N_COLS)
        def _(n):
            cols = pl.ds(pl.multiple_of(n * N_COLS, N_COLS), N_COLS)
            part = dot_nt(gg, wg[cols, :]) + dot_nt(ug, wu[cols, :])
            po[dyn, :, cols] = part[0:tile].astype(BF16)
            ps[dyn, :, cols] = part[tile:].astype(BF16)

    def sib_ps(s):
        return remote(ps.at[s], sp.at[s], s_ps.at[s], r_ps.at[s], sib)

    def add_rows(dst_slot, src):
        @pl.loop(0, K)
        def _(k):
            r = pl.ds(pl.multiple_of(k * rows, rows), rows)
            po[dst_slot, r, :] = (po[dst_slot, r, :].astype(F32) + src[r, :].astype(F32)).astype(BF16)

    load_g.wait()
    load_u.wait()
    from_sibling(0)
    forward((hi, e, 0), 0)

    def got1(k):
        slot, base = at1
        arrived(xr.at[slot, chunk(k, base)], r_ring.at[k])

    def got3(k):
        slot, base = at3
        arrived(xr.at[slot, chunk(k, base)], r_ring.at[K + k])

    def z1(k):
        return remote(xr.at[4, chunk(k)], xr.at[1, chunk(k)], s_z.at[k], r_z.at[k], zn)

    def z3(k):
        return remote(xr.at[4, chunk(k, tile)], xr.at[3, chunk(k)], s_z.at[K + k], r_z.at[K + k], zn)

    def opp1(k):
        slot, base = at1
        return remote(xr.at[slot, chunk(k, base)], xr.at[2, chunk(k)], s_opp.at[k], r_opp.at[k], yp)

    def opp3(k):
        slot, base = at3
        return remote(xr.at[slot, chunk(k, base)], xr.at[2, chunk(k)], s_opp.at[k], r_opp.at[k], ym)

    arrived(ch.at[4 - 3 * lo], r_cot.at[0])
    arrived(ch.at[5 - 2 * lo], r_cot.at[1])
    relay_dev = ((d + 2 * lo + 2 * lo) % 4, y_e)
    relay_dev = (lax.rem(d + 4 * lo, 4), y_e)
    cot_opp = remote(ch.at[4 - lo], ch.at[2], s_cot.at[2], r_cot.at[2], relay_dev)
    cot_opp.start()
    cot_z1 = remote(ch.at[4], ch.at[1], s_cot.at[3], r_cot.at[3], zn)
    cot_z3 = remote(ch.at[5], ch.at[3], s_cot.at[4], r_cot.at[4], zn)

    @pl.when(even)
    def _():
        cot_z1.start()
        cot_z3.start()

    got1(0)
    got3(K - 1)

    @pl.when(even)
    def _():
        z1(0).start()

    opp1(0).start()
    opp3(K - 1).start()
    input_grad(0)
    sib_ps(0).start()

    for k in range(1, K):
        got1(k)
        got3(K - 1 - k)

        @pl.when(even)
        def _():
            z1(k).start()

        if k < K // 2:
            opp1(k).start()
            opp3(K - 1 - k).start()

    @pl.when(even)
    def _():
        for k in range(K):
            z3(K - 1 - k).start()

    sib_ps(0).wait_recv()
    add_rows(0, sp.at[0])

    @pl.when(odd)
    def _():
        to_sibling(1)
        to_sibling(3)

    @pl.when(even)
    def _():
        cot_z1.wait_recv()
        for k in range(K):
            z1(k).wait_recv()
        to_sibling(1)

    from_sibling(1)
    forward((group_half(1), prev, 1), 1)
    input_grad(1)
    sib_ps(1).start()

    def zq(j, k):
        return remote(po.at[1 + 2 * j, chunk(k)], zc.at[j, chunk(k)], s_zc.at[K * j + k], r_zc.at[K * j + k], zp)

    def fin_of(j, k, src):
        return remote(src, fin.at[j, chunk(k)], s_fin.at[K * j + k], r_fin.at[K * j + k], ym if j == 0 else yp)

    def hid_of(j):
        dst = (1 - lo) if j == 0 else lo
        return remote(hv.at[1 + 2 * j], hb.at[dst], s_hid.at[j], r_hid.at[dst], prv)

    hid_of(0).start()

    third = 2 + lo
    fourth = 3 - lo

    @pl.when(even)
    def _():
        for k in range(K):
            arrived(xr.at[2, chunk(k)], r_opp.at[k])
        cot_opp.wait_recv()
        to_sibling(2)

    def dyn_from_sibling(s):
        arrived(xr.at[s, pl.ds(tile, tile)], r_sib.at[s])
        arrived(cs.at[s], r_cot.at[5 + s])

    sib_ps(1).wait_recv()
    add_rows(1, sp.at[1])

    @pl.when(even)
    def _():
        for k in range(K):
            zq(0, k).start()

    @pl.when(odd)
    def _():
        for k in range(K // 2, K):
            fin_of(0, k, po.at[1, chunk(k)]).start()

    dyn_from_sibling(third)
    gh_opp = 1 - hi
    gh_three = group_half(3)
    forward(
        (gh_opp * (1 - lo) + gh_three * lo, e * (1 - lo) + prev * lo, lo),
        third,
    )
    input_grad(third)

    def dyn_ps(s):
        return remote(ps.at[s], sp.at[s], s_ps.at[s], r_ps.at[s], sib)

    dyn_ps(third).start()

    @pl.when(odd)
    def _():
        hid_of(1).start()
        for k in range(K):
            arrived(xr.at[2, chunk(k)], r_opp.at[k])
        cot_opp.wait_recv()
        to_sibling(2)

    dyn_ps(third).wait_recv()
    add_rows(third, sp.at[third])

    hk = K // 2

    def m_of(j):
        r = chunk(j * hk, 0, hk)
        return remote(po.at[2, r], mv.at[j], s_m.at[j], r_m.at[j], ym if j == 0 else yp)

    @pl.when(even)
    def _():
        m_of(0).start()
        m_of(1).start()
        cot_z3.wait_recv()
        for k in range(K):
            z3(k).wait_recv()
        to_sibling(3)

    @pl.when(odd)
    def _():
        for k in range(hk):
            fin_of(1, k, po.at[3, chunk(k)]).start()

    dyn_from_sibling(fourth)
    forward(
        (gh_opp * lo + gh_three * (1 - lo), e * lo + prev * (1 - lo), 1 - lo),
        fourth,
    )
    input_grad(fourth)
    dyn_ps(fourth).start()

    @pl.when(even)
    def _():
        hid_of(1).start()

    dyn_ps(fourth).wait_recv()
    add_rows(fourth, sp.at[fourth])

    @pl.when(even)
    def _():
        for k in range(K):
            zq(1, k).start()

    @pl.when(odd)
    def _():
        m_of(0).start()
        m_of(1).start()

    m_of(0).wait_recv()
    m_of(1).wait_recv()

    def merge(dst, r, m_rows, m_slot):
        dst[r, :] = (dst[r, :].astype(F32) + mv[m_slot, m_rows, :].astype(F32)).astype(BF16)

    @pl.when(odd)
    def _():
        for k in range(hk):
            merge(po.at[1], chunk(k), chunk(k), 0)
            fin_of(0, k, po.at[1, chunk(k)]).start()
        for k in range(hk, K):
            merge(po.at[3], chunk(k), chunk(k - hk), 1)
            fin_of(1, k, po.at[3, chunk(k)]).start()

    @pl.when(even)
    def _():
        for k in range(K):
            zq(0, k).wait_recv()
            if k < hk:
                merge(zc.at[0], chunk(k), chunk(k), 0)
            fin_of(0, k, zc.at[0, chunk(k)]).start()

    @pl.loop(0, width // N_COLS)
    def _(n):
        cols = pl.ds(pl.multiple_of(n * N_COLS, N_COLS), N_COLS)
        x = xr[0:4, :, cols].reshape(8 * tile, N_COLS)
        grads = gu[...].reshape(8 * tile, half)
        total = dot_tn(x, grads) * (1.0 / tile)
        wgo[cols, :] = total[:, 0:quarter].astype(BF16)
        wuo[cols, :] = total[:, quarter:].astype(BF16)

    out_g = pltpu.make_async_copy(wgo, ggrad.at[0], l_wg.at[0])
    out_u = pltpu.make_async_copy(wuo, ugrad.at[0], l_wg.at[1])
    out_g.start()
    out_u.start()

    hid_copies = []
    for j in range(2):
        arrived(hb.at[j], r_hid.at[j])
        hv[2 * j, :, :] = (hv[2 * j].astype(F32) + hb[j].astype(F32)).astype(BF16)
        gh = hi if j == 0 else 1 - hi
        for part in range(2):
            group = gh * 2 + (c if part == 0 else 1 - c)
            cp = pltpu.make_async_copy(
                hv.at[2 * j, pl.ds(part * tile, tile)], hid.at[group], l_hid.at[2 * j + part]
            )
            cp.start()
            hid_copies.append(cp)

    @pl.when(even)
    def _():
        for k in range(K):
            zq(1, k).wait_recv()
            if k >= hk:
                merge(zc.at[1], chunk(k), chunk(k - hk), 1)
            fin_of(1, k, zc.at[1, chunk(k)]).start()

    dt_copies = []
    for k in range(K):
        arrived(fin.at[0, chunk(k)], r_fin.at[k])
        arrived(fin.at[1, chunk(k)], r_fin.at[K + k])
        r = chunk(k)
        po[0, r, :] = (po[0, r, :].astype(F32) + fin[0, r, :].astype(F32) + fin[1, r, :].astype(F32)).astype(BF16)
        cp = pltpu.make_async_copy(po.at[0, r], dtok.at[0, r], l_dt.at[k])
        cp.start()
        dt_copies.append(cp)

    for k in range(K):
        ring1(k, tok.at[0, chunk(k)], *to1).wait_send()
        ring3(k, tok.at[0, chunk(k)], *to3).wait_send()
        if k < hk:
            opp1(k).wait_send()
        else:
            opp3(k).wait_send()
        for j in range(2):
            sent(fin.at[j, chunk(k)], s_fin.at[K * j + k])
    cot1.wait_send()
    cot3.wait_send()
    cot_opp.wait_send()
    for s in range(4):
        sib_x(s).wait_send()
        sib_c(s).wait_send()
        sib_ps(s).wait_send()
    for j in range(2):
        hid_of(j).wait_send()
        m_of(j).wait_send()

    @pl.when(even)
    def _():
        cot_z1.wait_send()
        cot_z3.wait_send()
        for k in range(K):
            z1(k).wait_send()
            z3(k).wait_send()
            for j in range(2):
                zq(j, k).wait_send()

    out_g.wait()
    out_u.wait()
    for cp in hid_copies + dt_copies:
        cp.wait()


def per_device(experts, tokens, cotangent, gate_weights, tile_expert, w_gate, w_up):
    _, tile, width = tokens.shape
    quarter = w_gate.shape[2]
    groups = gate_weights.shape[0]
    half = 2 * quarter
    hbm = pl.BlockSpec(memory_space=pl.ANY)
    dma = pltpu.SemaphoreType.DMA
    return pl.pallas_call(
        functools.partial(kernel, experts),
        out_shape=(
            jax.ShapeDtypeStruct(tokens.shape, BF16),
            jax.ShapeDtypeStruct((groups, tile, quarter), BF16),
            jax.ShapeDtypeStruct(w_gate.shape, BF16),
            jax.ShapeDtypeStruct(w_up.shape, BF16),
        ),
        in_specs=[hbm, hbm, hbm, pl.BlockSpec(memory_space=pltpu.SMEM), hbm, hbm],
        out_specs=(hbm, hbm, hbm, hbm),
        scratch_shapes=[
            pltpu.VMEM((5, 2 * tile, width), BF16),
            pltpu.VMEM((6, tile, half), BF16),
            pltpu.VMEM((4, tile, quarter), BF16),
            pltpu.VMEM((2, groups, tile), F32),
            pltpu.VMEM((width, quarter), BF16),
            pltpu.VMEM((width, quarter), BF16),
            pltpu.VMEM((4, 2 * tile, half), BF16),
            pltpu.VMEM((4, 2 * tile, quarter), BF16),
            pltpu.VMEM((2, 2 * tile, quarter), BF16),
            pltpu.VMEM((4, tile, width), BF16),
            pltpu.VMEM((4, tile, width), BF16),
            pltpu.VMEM((4, tile, width), BF16),
            pltpu.VMEM((2, tile // 2, width), BF16),
            pltpu.VMEM((2, tile, width), BF16),
            pltpu.VMEM((2, tile, width), BF16),
            pltpu.VMEM((width, quarter), BF16),
            pltpu.VMEM((width, quarter), BF16),
            dma((2 * K,)), dma((2 * K,)),
            dma((K,)), dma((K,)),
            dma((2 * K,)), dma((2 * K,)),
            dma((4,)), dma((4,)),
            dma((9,)), dma((9,)),
            dma((4,)), dma((4,)),
            dma((2,)), dma((2,)),
            dma((2 * K,)), dma((2 * K,)),
            dma((2 * K,)), dma((2 * K,)),
            dma((2,)), dma((2,)),
            dma((4,)), dma((2,)), dma((4,)), dma((2,)), dma((K,)),
        ],
        compiler_params=pltpu.CompilerParams(
            collective_id=0, has_side_effects=True, vmem_limit_bytes=60 << 20
        ),
    )(tokens, cotangent, gate_weights, tile_expert, w_gate, w_up)


def solution(mesh):
    placed = (
        P("dp", "expert", None),
        P("dp", "expert", None),
        P(),
        P(),
        P("expert", None, "dp"),
        P("expert", None, "dp"),
    )
    return jax.shard_map(
        functools.partial(per_device, mesh.shape["expert"]),
        mesh=mesh,
        in_specs=placed,
        out_specs=(
            P("dp", "expert", None),
            P(None, "expert", "dp"),
            P("expert", None, "dp"),
            P("expert", None, "dp"),
        ),
        check_vma=False,
    )
```

```python
import functools

import jax
import jax.numpy as jnp
from jax import lax
from jax.experimental import pallas as pl
from jax.experimental.pallas import tpu as pltpu
from jax.sharding import PartitionSpec as P

MESH = pl.DeviceIdType.MESH
F32 = jnp.float32
BF16 = jnp.bfloat16
K = 4
N_COLS = 512


def dot_nn(a, b):
    return lax.dot_general(a, b, (((1,), (0,)), ((), ())), preferred_element_type=F32)


def dot_nt(a, b):
    return lax.dot_general(a, b, (((1,), (1,)), ((), ())), preferred_element_type=F32)


def dot_tn(a, b):
    return lax.dot_general(a, b, (((0,), (0,)), ((), ())), preferred_element_type=F32)


def kernel(
    experts,
    tok, cot, gw, te, wg_hbm, wu_hbm,
    dtok, hid, ggrad, ugrad,
    xr, ch, cs, gwv, wg, wu, gu, hv, hb, po, ps, sp, mv, zc, fin, rl,
    s_ring, r_relay, r_x, s_opp, r_opp, s_z, s_sib, r_sib,
    s_cot, r_cot, s_ps, r_ps, s_m, r_m, s_zc, r_zc, s_fin, r_fin, s_leg, r_leg, r_fin2, s_hid, r_hid,
    l_in, l_gw,
):
    tile = tok.shape[1]
    width = tok.shape[2]
    quarter = wg_hbm.shape[2]
    half = 2 * quarter
    rows = tile // K
    d = lax.axis_index("dp")
    e = lax.axis_index("expert")
    hi, c = d // 2, d % 2
    lo = e % 2
    prev = (e + experts - 1) % experts

    y_e = e + 1 - 2 * lo
    yp = ((d + 2 * lo) % 4, y_e)
    ym = ((d + 2 * (1 - lo)) % 4, y_e)
    opp = ((d + 2) % 4, e)
    sib = (d + 1 - 2 * c, e)
    zn = (d, (e + 2) % experts)
    zp = (d, (e + experts - 2) % experts)
    nxt = (d, (e + 1) % experts)
    nx2 = ((d + 2) % 4, (e + 1) % experts)
    prv = (d, prev)
    pr2 = ((d + 2) % 4, prev)

    def remote(src, dst, send, recv, dev):
        return pltpu.make_async_remote_copy(
            src_ref=src, dst_ref=dst, send_sem=send, recv_sem=recv, device_id=dev, device_id_type=MESH
        )

    def arrived(dst, recv):
        remote(dst, dst, s_m.at[0], recv, sib).wait_recv()

    def sent(src, send):
        remote(src, src, send, r_m.at[0], sib).wait_send()

    def chunk(k, base=0, count=1):
        return pl.ds(base + k * rows, rows * count)

    even = lo == 0
    odd = lo == 1

    own_x = pltpu.make_async_copy(tok.at[0], xr.at[0, pl.ds(0, tile)], l_in.at[0])
    own_c = pltpu.make_async_copy(
        cot.at[0, :, pl.ds(pl.multiple_of(hi * half, half), half)], ch.at[0], l_in.at[1]
    )
    load_g = pltpu.make_async_copy(wg_hbm.at[0], wg, l_in.at[2])
    load_u = pltpu.make_async_copy(wu_hbm.at[0], wu, l_in.at[3])
    gw_own = pltpu.make_async_copy(gw.at[:, pl.ds(pl.multiple_of(e * tile, tile), tile)], gwv.at[0], l_gw.at[0])
    gw_prev = pltpu.make_async_copy(
        gw.at[:, pl.ds(pl.multiple_of(prev * tile, tile), tile)], gwv.at[1], l_gw.at[1]
    )
    own_x.start()
    own_c.start()
    load_g.start()
    load_u.start()
    gw_own.start()
    gw_prev.start()

    barrier = pltpu.get_barrier_semaphore()

    def greet(devices):
        for dev in devices:
            pl.semaphore_signal(barrier, inc=1, device_id=dev, device_id_type=MESH)
        pl.semaphore_wait(barrier, 7)

    mine = pl.ds(pl.multiple_of(c * quarter, quarter), quarter)
    other = pl.ds(pl.multiple_of((1 - c) * quarter, quarter), quarter)

    def cot_half(h, slot, i, dev):
        h = lax.rem(h, 2)
        return remote(
            cot.at[0, :, pl.ds(pl.multiple_of(h * half, half), half)],
            ch.at[slot], s_cot.at[i], r_cot.at[slot], dev,
        )

    def tile_to(k, slot, base, i, recv, dev):
        return remote(tok.at[0, chunk(k)], xr.at[slot, chunk(k, base)], s_ring.at[i], recv, dev)

    hk = K // 2
    first = range(hk)
    second = range(hk, K)
    up_order = list(range(K))
    down_order = up_order[::-1]

    def even_ring1(k):
        return tile_to(k, 1, 0, k, r_x.at[k], yp)

    def even_ring3(k):
        return tile_to(k, 3, 0, K + k, r_x.at[K + k], ym)

    even_cots = [cot_half(hi, 1, 0, yp), cot_half(hi + 1, 3, 1, ym), cot_half(hi + 1, 2, 2, opp)]

    def odd_ring(k):
        if k < hk:
            return tile_to(k, 4, 0, k, r_relay.at[k], yp)
        return tile_to(k, 4, tile, k, r_relay.at[k], ym)

    def odd_up(k):
        if k < hk:
            return tile_to(k, 3, 0, K + k, r_x.at[K + k], nxt)
        return tile_to(k, 1, 0, K + k, r_x.at[k], nx2)

    odd_cots = [cot_half(hi, 3, 0, nxt), cot_half(hi + 1, 1, 1, nx2), cot_half(hi + 1, 2, 2, opp)]

    @pl.when(even)
    def _():
        greet((yp, ym, sib, zn, zp, opp, prv, pr2))
        for k in range(K):
            even_ring1(up_order[k]).start()
            even_ring3(down_order[k]).start()
            if k == 1:
                for copy in even_cots:
                    copy.start()

    @pl.when(odd)
    def _():
        greet((yp, ym, sib, opp, zn, nxt))
        for k in range(hk):
            odd_ring(up_order[k]).start()
            odd_ring(down_order[k]).start()
            odd_up(hk + k).start()
            odd_up(hk - 1 - k).start()
        for copy in odd_cots:
            copy.start()

    def sib_x(s):
        return remote(xr.at[s, pl.ds(0, tile)], xr.at[s, pl.ds(tile, tile)], s_sib.at[s], r_sib.at[s], sib)

    def sib_c(s):
        return remote(ch.at[s, :, other], cs.at[s], s_cot.at[3 + s], r_cot.at[4 + s], sib)

    def to_sibling(s):
        sib_x(s).start()
        sib_c(s).start()

    def from_sibling(s):
        sib_x(s).wait_recv()
        sib_c(s).wait_recv()

    own_x.wait()
    own_c.wait()
    to_sibling(0)

    eye = lax.broadcasted_iota(jnp.int32, (tile, tile), 0) == lax.broadcasted_iota(jnp.int32, (tile, tile), 1)
    gw_own.wait()
    gw_prev.wait()

    def scale_of(group, place, which):
        line = gwv[which, pl.ds(group, 1), :]
        routed = jnp.where(te[group, place] == e, jnp.float32(1.0), jnp.float32(0.0))
        spread = jnp.where(eye, jnp.broadcast_to(line, (tile, tile)), jnp.float32(0.0))
        return jnp.sum(spread, axis=1, keepdims=True) * routed

    def group_half(s):
        return (hi, (hi + 1 - lo) % 2, 1 - hi, (hi + lo) % 2)[s]

    def forward(s):
        gh = group_half(s)
        place, which = (e, 0) if s % 2 == 0 else (prev, 1)
        x = xr[s]
        gate = dot_nn(x, wg[...])
        up = dot_nn(x, wu[...])
        for part in range(2):
            group = gh * 2 + (c if part == 0 else 1 - c)
            w = scale_of(group, place, which)
            r = slice(part * tile, (part + 1) * tile)
            dh = (ch[s, :, mine] if part == 0 else cs[s]).astype(F32)
            g, u = gate[r], up[r]
            sg = jax.nn.sigmoid(g)
            act = g * sg
            hv[s, r, :] = ((w * act) * u).astype(BF16)
            ag = w * dh
            gu[s, r, 0:quarter] = (ag * u * sg * (1.0 + g * (1.0 - sg))).astype(BF16)
            gu[s, r, quarter:half] = (ag * act).astype(BF16)

    def input_grad(dyn):
        gg = gu[dyn, :, 0:quarter]
        ug = gu[dyn, :, quarter:half]

        @pl.loop(0, width // N_COLS)
        def _(n):
            cols = pl.ds(pl.multiple_of(n * N_COLS, N_COLS), N_COLS)
            part = dot_nt(gg, wg[cols, :]) + dot_nt(ug, wu[cols, :])
            po[dyn, :, cols] = part[0:tile].astype(BF16)
            ps[dyn, :, cols] = part[tile:].astype(BF16)

    def sib_ps(s):
        return remote(ps.at[s], sp.at[s], s_ps.at[s], r_ps.at[s], sib)

    def contribution(s):
        sib_ps(s).wait_recv()

        @pl.loop(0, K)
        def _(k):
            r = pl.ds(pl.multiple_of(k * rows, rows), rows)
            po[s, r, :] = (po[s, r, :].astype(F32) + sp[s, r, :].astype(F32)).astype(BF16)

    def relay_z(k):
        if k < hk:
            return remote(xr.at[4, chunk(k)], xr.at[1, chunk(k)], s_z.at[k], r_x.at[k], zn)
        return remote(xr.at[4, chunk(k, tile)], xr.at[3, chunk(k)], s_z.at[k], r_x.at[K + k], zn)

    def relay_opp(k, src_slot, base):
        src = xr.at[src_slot, chunk(k, base)]
        return remote(src, xr.at[2, chunk(k)], s_opp.at[k], r_opp.at[k], yp if k < hk else ym)

    def even_opp(k):
        return relay_opp(k, 4, 0 if k < hk else tile)

    def odd_opp(k):
        return relay_opp(k, 1 if k < hk else 3, 0)

    def got_relay(k):
        arrived(xr.at[4, chunk(k, 0 if k < hk else tile)], r_relay.at[k])

    def got_x(s, k):
        arrived(xr.at[s, chunk(k)], r_x.at[(0 if s == 1 else K) + k])

    def got_cot(s):
        arrived(ch.at[s], r_cot.at[s])

    def got_opp():
        for k in range(K):
            arrived(xr.at[2, chunk(k)], r_opp.at[k])
        got_cot(2)

    def m_of(j):
        r = chunk(j * hk, 0, hk)
        return remote(po.at[2, r], mv.at[j], s_m.at[j], r_m.at[j], ym if j == 0 else yp)

    def fin_of(j, k, src):
        return remote(src, fin.at[j, chunk(k)], s_fin.at[K * j + k], r_fin.at[K * j + k], ym if j == 0 else yp)

    def zq(j, k):
        return remote(po.at[1 + 2 * j, chunk(k)], zc.at[j, chunk(k - j * hk)], s_zc.at[k], r_zc.at[k], zp)

    def leg(j):
        r = chunk((1 - j) * hk, 0, hk)
        return remote(po.at[1 + 2 * j, r], rl.at[j], s_leg.at[j], r_leg.at[j], ym if j == 0 else yp)

    def leg_on(j):
        r = chunk((1 - j) * hk, 0, hk)
        return remote(rl.at[j], fin.at[j, r], s_leg.at[j], r_fin2.at[j], zp)

    def hid_of(j):
        dst = (1 - lo) if j == 0 else lo
        return remote(hv.at[1 + 2 * j], hb.at[dst], s_hid.at[j], r_hid.at[dst], prv)

    def merge(dst, r, m_rows, m_slot):
        dst[r, :] = (dst[r, :].astype(F32) + mv[m_slot, m_rows, :].astype(F32)).astype(BF16)

    def weight_grads():
        @pl.loop(0, width // N_COLS)
        def _(n):
            cols = pl.ds(pl.multiple_of(n * N_COLS, N_COLS), N_COLS)
            x = xr[0:4, :, cols].reshape(8 * tile, N_COLS)
            grads = gu[...].reshape(8 * tile, half)
            total = dot_tn(x, grads) * (1.0 / tile)
            ggrad[0, cols, :] = total[:, 0:quarter].astype(BF16)
            ugrad[0, cols, :] = total[:, quarter:].astype(BF16)

    def hidden_out():
        for j in range(2):
            arrived(hb.at[j], r_hid.at[j])
            gh = hi if j == 0 else 1 - hi
            for part in range(2):
                group = gh * 2 + (c if part == 0 else 1 - c)
                r = slice(part * tile, (part + 1) * tile)
                hid[group, :, :] = (hv[2 * j, r, :].astype(F32) + hb[j, r, :].astype(F32)).astype(BF16)

    def total(k):
        r = chunk(k)
        dtok[0, r, :] = (po[0, r, :].astype(F32) + fin[0, r, :].astype(F32) + fin[1, r, :].astype(F32)).astype(BF16)

    load_g.wait()
    load_u.wait()

    @pl.when(even)
    def _():
        from_sibling(0)
        forward(0)
        for k in (0, K - 1):
            got_relay(k)
            relay_z(k).start()
            even_opp(k).start()
        input_grad(0)
        sib_ps(0).start()
        for k in (1, K - 2):
            got_relay(k)
            relay_z(k).start()
            even_opp(k).start()
        contribution(0)
        for s in (1, 3):
            got_cot(s)
            for k in range(K):
                got_x(s, k)
            to_sibling(s)
        from_sibling(1)
        forward(1)
        input_grad(1)
        sib_ps(1).start()
        hid_of(0).start()
        from_sibling(3)
        forward(3)
        hid_of(1).start()
        contribution(1)
        leg(0).start()
        for k in first:
            zq(0, k).start()
        input_grad(3)
        sib_ps(3).start()
        got_opp()
        to_sibling(2)
        contribution(3)
        leg(1).start()
        for k in second:
            zq(1, k).start()
        from_sibling(2)
        forward(2)
        input_grad(2)
        sib_ps(2).start()
        contribution(2)
        m_of(0).start()
        m_of(1).start()
        for j in range(2):
            m_of(j).wait_recv()
            for i in range(hk):
                k = j * hk + i
                zq(j, k).wait_recv()
                merge(zc.at[j], chunk(i), chunk(i), j)
                fin_of(j, k, zc.at[j, chunk(i)]).start()
        weight_grads()
        hidden_out()
        for k in range(K):
            for j in range(2):
                arrived(fin.at[j, chunk(k)], r_fin.at[K * j + k])
            total(k)
        for k in range(K):
            even_ring1(k).wait_send()
            even_ring3(k).wait_send()
            relay_z(k).wait_send()
            even_opp(k).wait_send()
            zq(k // hk, k).wait_send()
            fin_of(k // hk, k, zc.at[k // hk, chunk(k % hk)]).wait_send()
        for copy in even_cots:
            copy.wait_send()
        for j in range(2):
            leg(j).wait_send()

    @pl.when(odd)
    def _():
        from_sibling(0)
        forward(0)
        for k in (0, K - 1):
            got_x(1 if k < hk else 3, k)
            odd_opp(k).start()
        input_grad(0)
        sib_ps(0).start()
        for k in (1, K - 2):
            got_x(1 if k < hk else 3, k)
            odd_opp(k).start()
        contribution(0)
        for s in (1, 3):
            got_cot(s)
            for k in second if s == 1 else first:
                got_x(s, k)
            to_sibling(s)
        from_sibling(1)
        forward(1)
        input_grad(1)
        sib_ps(1).start()
        hid_of(0).start()
        from_sibling(3)
        forward(3)
        hid_of(1).start()
        contribution(1)
        for k in second:
            fin_of(0, k, po.at[1, chunk(k)]).start()
        input_grad(3)
        sib_ps(3).start()
        got_opp()
        to_sibling(2)
        contribution(3)
        for k in first:
            fin_of(1, k, po.at[3, chunk(k)]).start()
        from_sibling(2)
        forward(2)
        input_grad(2)
        sib_ps(2).start()
        contribution(2)
        m_of(0).start()
        m_of(1).start()
        for j in range(2):
            leg(j).wait_recv()
            leg_on(j).start()
        for j in range(2):
            m_of(j).wait_recv()
            for i in range(hk):
                k = j * hk + i
                src = po.at[1 + 2 * j]
                merge(src, chunk(k), chunk(i), j)
                fin_of(j, k, src.at[chunk(k)]).start()
        weight_grads()
        hidden_out()
        for j in range(2):
            r = chunk((1 - j) * hk, 0, hk)
            arrived(fin.at[j, r], r_fin2.at[j])
        for k in range(K):
            arrived(fin.at[k // hk, chunk(k)], r_fin.at[K * (k // hk) + k])
            total(k)
        for k in range(K):
            odd_ring(k).wait_send()
            odd_up(k).wait_send()
            odd_opp(k).wait_send()
            for j in range(2):
                fin_of(j, k, po.at[1 + 2 * j, chunk(k)]).wait_send()
        for copy in odd_cots:
            copy.wait_send()
        for j in range(2):
            leg_on(j).wait_send()

    for s in range(4):
        sib_x(s).wait_send()
        sib_c(s).wait_send()
        sib_ps(s).wait_send()
    for j in range(2):
        hid_of(j).wait_send()
        m_of(j).wait_send()


def store(*refs):
    count = len(refs) // 2
    sem = refs[-1]
    copies = [pltpu.make_async_copy(refs[i], refs[count + i], sem.at[i]) for i in range(count)]
    for copy in copies:
        copy.start()
    for copy in copies:
        copy.wait()


def per_device(experts, tokens, cotangent, gate_weights, tile_expert, w_gate, w_up):
    _, tile, width = tokens.shape
    quarter = w_gate.shape[2]
    groups = gate_weights.shape[0]
    half = 2 * quarter
    hbm = pl.BlockSpec(memory_space=pltpu.HBM)
    dma = pltpu.SemaphoreType.DMA
    vmem = pl.BlockSpec(memory_space=pltpu.VMEM)
    shapes = (tokens.shape, (groups, tile, quarter), w_gate.shape, w_up.shape)
    parts = pl.pallas_call(
        functools.partial(kernel, experts),
        out_shape=tuple(pltpu.VMEM(shape, BF16) for shape in shapes),
        in_specs=[hbm, hbm, hbm, pl.BlockSpec(memory_space=pltpu.SMEM), hbm, hbm],
        out_specs=(vmem, vmem, vmem, vmem),
        scratch_shapes=[
            pltpu.VMEM((5, 2 * tile, width), BF16),
            pltpu.VMEM((4, tile, half), BF16),
            pltpu.VMEM((4, tile, quarter), BF16),
            pltpu.VMEM((2, groups, tile), F32),
            pltpu.VMEM((width, quarter), BF16),
            pltpu.VMEM((width, quarter), BF16),
            pltpu.VMEM((4, 2 * tile, half), BF16),
            pltpu.VMEM((4, 2 * tile, quarter), BF16),
            pltpu.VMEM((2, 2 * tile, quarter), BF16),
            pltpu.VMEM((4, tile, width), BF16),
            pltpu.VMEM((4, tile, width), BF16),
            pltpu.VMEM((4, tile, width), BF16),
            pltpu.VMEM((2, tile // 2, width), BF16),
            pltpu.VMEM((2, tile // 2, width), BF16),
            pltpu.VMEM((2, tile, width), BF16),
            pltpu.VMEM((2, tile // 2, width), BF16),
            dma((2 * K,)), dma((K,)), dma((2 * K,)),
            dma((K,)), dma((K,)),
            dma((K,)),
            dma((4,)), dma((4,)),
            dma((7,)), dma((8,)),
            dma((4,)), dma((4,)),
            dma((2,)), dma((2,)),
            dma((K,)), dma((K,)),
            dma((2 * K,)), dma((2 * K,)),
            dma((2,)), dma((2,)), dma((2,)),
            dma((2,)), dma((2,)),
            dma((4,)), dma((2,)),
        ],
        compiler_params=pltpu.CompilerParams(
            collective_id=0, has_side_effects=True, vmem_limit_bytes=62_192_000
        ),
    )(tokens, cotangent, gate_weights, tile_expert, w_gate, w_up)
    return pl.pallas_call(
        store,
        out_shape=tuple(jax.ShapeDtypeStruct(shape, BF16) for shape in shapes),
        in_specs=[pl.BlockSpec(memory_space=pl.ANY)] * 4,
        out_specs=(hbm, hbm, hbm, hbm),
        scratch_shapes=[dma((4,))],
        compiler_params=pltpu.CompilerParams(vmem_limit_bytes=1 << 20),
    )(*parts)


def solution(mesh):
    placed = (
        P("dp", "expert", None),
        P("dp", "expert", None),
        P(),
        P(),
        P("expert", None, "dp"),
        P("expert", None, "dp"),
    )
    return jax.shard_map(
        functools.partial(per_device, mesh.shape["expert"]),
        mesh=mesh,
        in_specs=placed,
        out_specs=(
            P("dp", "expert", None),
            P(None, "expert", "dp"),
            P("expert", None, "dp"),
            P("expert", None, "dp"),
        ),
        check_vma=False,
    )
```

```python
import functools

import jax
import jax.numpy as jnp
from jax import lax
from jax.experimental import pallas as pl
from jax.experimental.pallas import tpu as pltpu
from jax.sharding import PartitionSpec as P

MESH = pl.DeviceIdType.MESH
F32 = jnp.float32
BF16 = jnp.bfloat16
K = 4
N_COLS = 512


def dot_nn(a, b):
    return lax.dot_general(a, b, (((1,), (0,)), ((), ())), preferred_element_type=F32)


def dot_nt(a, b):
    return lax.dot_general(a, b, (((1,), (1,)), ((), ())), preferred_element_type=F32)


def dot_tn(a, b):
    return lax.dot_general(a, b, (((0,), (0,)), ((), ())), preferred_element_type=F32)


def kernel(
    experts,
    tok, cot, gw, te, wg_hbm, wu_hbm,
    dtok, hid, ggrad, ugrad,
    xr, xrelay, ch, cs, gwv, wg, wu, gu, hv, hb, po, ps, sp, mv, zc, fin, rl,
    s_ring, r_relay, r_x, s_opp, r_opp, s_z, s_sib, r_sib, s_cot, r_cot, s_sc, r_sc,
    s_ps, r_ps, s_m, r_m, s_zc, r_zc, s_fin, r_fin, s_leg, r_leg, s_hid, r_hid,
    l_in, l_gw,
):
    tile = tok.shape[1]
    width = tok.shape[2]
    quarter = wg_hbm.shape[2]
    half = 2 * quarter
    rows = tile // K
    d = lax.axis_index("dp")
    e = lax.axis_index("expert")
    hi, c = d // 2, d % 2
    lo = e % 2
    prev = (e + experts - 1) % experts

    y_e = e + 1 - 2 * lo
    yp = ((d + 2 * lo) % 4, y_e)
    ym = ((d + 2 * (1 - lo)) % 4, y_e)
    opp = ((d + 2) % 4, e)
    sib = (d + 1 - 2 * c, e)
    zn = (d, (e + 2) % experts)
    zp = (d, (e + experts - 2) % experts)
    nxt = (d, (e + 1) % experts)
    nx2 = ((d + 2) % 4, (e + 1) % experts)
    prv = (d, prev)
    pr2 = ((d + 2) % 4, prev)

    def remote(src, dst, send, recv, dev):
        return pltpu.make_async_remote_copy(
            src_ref=src, dst_ref=dst, send_sem=send, recv_sem=recv, device_id=dev, device_id_type=MESH
        )

    def arrived(dst, recv):
        remote(dst, dst, s_m.at[0], recv, sib).wait_recv()

    def sent(src, send):
        remote(src, src, send, r_m.at[0], sib).wait_send()

    def chunk(k, base=0, count=1):
        return pl.ds(base + k * rows, rows * count)

    even = lo == 0
    odd = lo == 1

    own_x = pltpu.make_async_copy(tok.at[0], xr.at[0, pl.ds(0, tile)], l_in.at[0])
    own_c = pltpu.make_async_copy(
        cot.at[0, :, pl.ds(pl.multiple_of(hi * half, half), half)], ch.at[0], l_in.at[1]
    )
    load_g = pltpu.make_async_copy(wg_hbm.at[0], wg, l_in.at[2])
    load_u = pltpu.make_async_copy(wu_hbm.at[0], wu, l_in.at[3])
    gw_own = pltpu.make_async_copy(gw.at[:, pl.ds(pl.multiple_of(e * tile, tile), tile)], gwv.at[0], l_gw.at[0])
    gw_prev = pltpu.make_async_copy(
        gw.at[:, pl.ds(pl.multiple_of(prev * tile, tile), tile)], gwv.at[1], l_gw.at[1]
    )
    own_x.start()
    own_c.start()
    load_g.start()
    load_u.start()
    gw_own.start()
    gw_prev.start()

    barrier = pltpu.get_barrier_semaphore()

    def greet(devices):
        for dev in devices:
            pl.semaphore_signal(barrier, inc=1, device_id=dev, device_id_type=MESH)
        pl.semaphore_wait(barrier, 7)

    mine = pl.ds(pl.multiple_of(c * quarter, quarter), quarter)
    other = pl.ds(pl.multiple_of((1 - c) * quarter, quarter), quarter)

    hk = K // 2
    pairs = [(i, K - 1 - i) for i in range(hk)]
    order = [k for pair in pairs for k in pair]
    low, high = pl.ds(0, tile // 2), pl.ds(tile // 2, tile // 2)

    def cot_to(h, r, slot, i, recv, dev):
        h = lax.rem(h, 2)
        return remote(
            cot.at[0, r, pl.ds(pl.multiple_of(h * half, half), half)],
            ch.at[slot, r], s_cot.at[i], r_cot.at[recv], dev,
        )

    all_rows = pl.ds(0, tile)
    cot_opp = cot_to(hi + 1, all_rows, 2, 4, 4, opp)

    def x_to(k, slot, i, dev):
        return remote(
            tok.at[0, chunk(k)], xr.at[slot, chunk(k)], s_ring.at[i], r_x.at[(0 if slot == 1 else K) + k], dev
        )

    def even_first(k):
        return x_to(k, 1, k, yp if k < hk else ym)

    def even_last(k):
        return x_to(k, 3, K + k, ym if k < hk else yp)

    even_cots = [
        cot_to(hi, low, 1, 0, 0, yp), cot_to(hi + 1, high, 1, 1, 1, ym),
        cot_to(hi + 1, low, 3, 2, 2, ym), cot_to(hi, high, 3, 3, 3, yp),
    ]

    def odd_ring(k):
        return remote(
            tok.at[0, chunk(k)], xrelay.at[chunk(k)], s_ring.at[k], r_relay.at[k], yp if k < hk else ym
        )

    def odd_up(k):
        return x_to(k, 3, K + k, nxt if k < hk else nx2)

    odd_cots = [
        cot_to(hi + 1, low, 1, 0, 0, nx2), cot_to(hi, high, 1, 1, 1, nxt),
        cot_to(hi, low, 3, 2, 2, nxt), cot_to(hi + 1, high, 3, 3, 3, nx2),
    ]

    @pl.when(even)
    def _():
        greet((yp, ym, sib, zn, zp, opp, prv, pr2))
        for k in order:
            even_first(k).start()

    @pl.when(odd)
    def _():
        greet((yp, ym, sib, opp, zn, nxt))
        for k in order:
            odd_ring(k).start()

    def sib_x(s, k):
        return remote(
            xr.at[s, chunk(k)], xr.at[s, chunk(k, tile)], s_sib.at[K * s + k], r_sib.at[K * s + k], sib
        )

    def sib_c(s):
        return remote(ch.at[s, :, other], cs.at[s], s_sc.at[s], r_sc.at[s], sib)

    def from_sibling(s):
        for k in range(K):
            sib_x(s, k).wait_recv()
        sib_c(s).wait_recv()

    own_x.wait()
    own_c.wait()
    for k in range(K):
        sib_x(0, k).start()
    sib_c(0).start()

    eye = lax.broadcasted_iota(jnp.int32, (tile, tile), 0) == lax.broadcasted_iota(jnp.int32, (tile, tile), 1)
    first_lanes = lax.broadcasted_iota(jnp.int32, (1, tile), 1) < tile // 2
    gw_own.wait()
    gw_prev.wait()

    gh_one = (hi + 1 - lo) % 2
    gh_three = (hi + lo) % 2

    def weights_of(gh, core, place, which):
        group = gh * 2 + core
        routed = jnp.where(te[group, place] == e, jnp.float32(1.0), jnp.float32(0.0))
        return gwv[which, pl.ds(group, 1), :] * routed

    def scale_of(s, core):
        if s % 2 == 0:
            line = weights_of(hi if s == 0 else 1 - hi, core, e, 0)
        else:
            one = weights_of(gh_one, core, prev, 1)
            three = weights_of(gh_three, core, prev, 1)
            line = jnp.where(first_lanes, one, three) if s == 1 else jnp.where(first_lanes, three, one)
        spread = jnp.where(eye, jnp.broadcast_to(line, (tile, tile)), jnp.float32(0.0))
        return jnp.sum(spread, axis=1, keepdims=True)

    def forward(s):
        x = xr[s]
        gate = dot_nn(x, wg[...])
        up = dot_nn(x, wu[...])
        for part in range(2):
            w = scale_of(s, c if part == 0 else 1 - c)
            r = slice(part * tile, (part + 1) * tile)
            dh = (ch[s, :, mine] if part == 0 else cs[s]).astype(F32)
            g, u = gate[r], up[r]
            sg = jax.nn.sigmoid(g)
            act = g * sg
            hv[s, r, :] = ((w * act) * u).astype(BF16)
            ag = w * dh
            gu[s, r, 0:quarter] = (ag * u * sg * (1.0 + g * (1.0 - sg))).astype(BF16)
            gu[s, r, quarter:half] = (ag * act).astype(BF16)

    def sib_ps(s):
        return remote(ps.at[s], sp.at[s], s_ps.at[s], r_ps.at[s], sib)

    def input_grad(s):
        gg = gu[s, :, 0:quarter]
        ug = gu[s, :, quarter:half]

        @pl.loop(0, width // N_COLS)
        def _(n):
            cols = pl.ds(pl.multiple_of(n * N_COLS, N_COLS), N_COLS)
            part = dot_nt(gg, wg[cols, :]) + dot_nt(ug, wu[cols, :])
            po[s, :, cols] = part[0:tile].astype(BF16)
            ps[s, :, cols] = part[tile:].astype(BF16)

        sib_ps(s).start()

    def contribution(s, send=None):
        sib_ps(s).wait_recv()
        for k in order:
            r = chunk(k)
            po[s, r, :] = (po[s, r, :].astype(F32) + sp[s, r, :].astype(F32)).astype(BF16)
            if send is not None:
                send(k).start()

    def relay_z(k):
        return remote(xrelay.at[chunk(k)], xr.at[1, chunk(k)], s_z.at[k], r_x.at[k], zn)

    def relay_opp(k, src):
        return remote(src, xr.at[2, chunk(k)], s_opp.at[k], r_opp.at[k], yp if k < hk else ym)

    def even_opp(k):
        return relay_opp(k, xrelay.at[chunk(k)])

    def odd_opp(k):
        return relay_opp(k, xr.at[1, chunk(k)])

    def got_relay(k):
        arrived(xrelay.at[chunk(k)], r_relay.at[k])

    def got_cot(s):
        if s == 2:
            arrived(ch.at[2], r_cot.at[4])
        else:
            arrived(ch.at[s, low], r_cot.at[s - 1])
            arrived(ch.at[s, high], r_cot.at[s])
        sib_c(s).start()

    def got(s, k):
        arrived(xr.at[s, chunk(k)], r_opp.at[k] if s == 2 else r_x.at[(0 if s == 1 else K) + k])
        sib_x(s, k).start()

    def got_all(s):
        got_cot(s)
        for k in order:
            got(s, k)

    def m_of(k):
        return remote(po.at[2, chunk(k)], mv.at[chunk(k)], s_m.at[k], r_m.at[k], ym if k < hk else yp)

    def fin_a(k, src):
        j = 0 if k < hk else 1
        return remote(
            src.at[chunk(k)], fin.at[j, chunk(k)], s_fin.at[k], r_fin.at[K * j + k], ym if k < hk else yp
        )

    def fin_b(k):
        j = 1 if k < hk else 0
        return remote(
            po.at[3, chunk(k)], fin.at[j, chunk(k)], s_fin.at[K + k], r_fin.at[K * j + k], yp if k < hk else ym
        )

    def zq(k):
        return remote(po.at[1, chunk(k)], zc.at[chunk(k)], s_zc.at[k], r_zc.at[k], zp)

    def leg(k):
        return remote(po.at[3, chunk(k)], rl.at[chunk(k)], s_leg.at[k], r_leg.at[k], yp if k < hk else ym)

    def leg_on(k):
        j = 1 if k < hk else 0
        return remote(rl.at[chunk(k)], fin.at[j, chunk(k)], s_leg.at[k], r_fin.at[K * j + k], zp)

    def hid_of(j):
        return remote(hv.at[1 + 2 * j], hb.at[j], s_hid.at[j], r_hid.at[j], prv)

    def merge(dst, k):
        r = chunk(k)
        dst[r, :] = (dst[r, :].astype(F32) + mv[r, :].astype(F32)).astype(BF16)

    def weight_grads():
        @pl.loop(0, width // N_COLS)
        def _(n):
            cols = pl.ds(pl.multiple_of(n * N_COLS, N_COLS), N_COLS)
            x = xr[:, :, cols].reshape(8 * tile, N_COLS)
            grads = gu[...].reshape(8 * tile, half)
            total = dot_tn(x, grads) * (1.0 / tile)
            ggrad[0, cols, :] = total[:, 0:quarter].astype(BF16)
            ugrad[0, cols, :] = total[:, quarter:].astype(BF16)

    def hidden_out(first):
        for j in range(2):
            hid_of(j).wait_recv()
        for slot in (0, 2):
            gh = hi if slot == 0 else 1 - hi
            lead = first if slot == 0 else 1 - first
            for part in range(2):
                group = gh * 2 + (c if part == 0 else 1 - c)
                for i in range(2):
                    r = slice(part * tile + i * (tile // 2), part * tile + (i + 1) * (tile // 2))
                    back = hb[lead if i == 0 else 1 - lead, r, :]
                    hid[group, i * (tile // 2) : (i + 1) * (tile // 2), :] = (
                        hv[slot, r, :].astype(F32) + back.astype(F32)
                    ).astype(BF16)

    def totals():
        for k in order:
            for j in range(2):
                arrived(fin.at[j, chunk(k)], r_fin.at[K * j + k])
            r = chunk(k)
            dtok[0, r, :] = (po[0, r, :].astype(F32) + fin[0, r, :].astype(F32) + fin[1, r, :].astype(F32)).astype(
                BF16
            )

    load_g.wait()
    load_u.wait()

    @pl.when(even)
    def _():
        for k in [k for i in range(hk) for k in (hk + i, hk - 1 - i)]:
            even_last(k).start()
        for copy in even_cots[2:]:
            copy.start()
        for copy in even_cots[:2]:
            copy.start()
        cot_opp.start()
        from_sibling(0)
        forward(0)
        for k in order[:hk]:
            got_relay(k)
            relay_z(k).start()
            even_opp(k).start()
        input_grad(0)
        for k in order[hk:]:
            got_relay(k)
            relay_z(k).start()
            even_opp(k).start()
        contribution(0)
        got_all(3)
        from_sibling(3)
        forward(3)
        hid_of(1).start()
        input_grad(3)
        got_all(1)
        contribution(3, leg)
        from_sibling(1)
        forward(1)
        hid_of(0).start()
        input_grad(1)
        got_all(2)
        contribution(1, zq)
        from_sibling(2)
        forward(2)
        input_grad(2)
        contribution(2, m_of)
        for k in order:
            m_of(k).wait_recv()
            zq(k).wait_recv()
            merge(zc, k)
            fin_a(k, zc).start()
        weight_grads()
        hidden_out(0)
        totals()
        for k in range(K):
            even_first(k).wait_send()
            even_last(k).wait_send()
            relay_z(k).wait_send()
            even_opp(k).wait_send()
            zq(k).wait_send()
            leg(k).wait_send()
            fin_a(k, zc).wait_send()
        for copy in even_cots:
            copy.wait_send()

    @pl.when(odd)
    def _():
        for k in order:
            odd_up(k).start()
        for copy in odd_cots[2:]:
            copy.start()
        for copy in odd_cots[:2]:
            copy.start()
        cot_opp.start()
        from_sibling(0)
        forward(0)
        for k in order[:hk]:
            got(1, k)
            odd_opp(k).start()
        input_grad(0)
        for k in order[hk:]:
            got(1, k)
            odd_opp(k).start()
        got_cot(1)
        contribution(0)
        from_sibling(1)
        forward(1)
        hid_of(0).start()
        input_grad(1)
        got_all(3)
        contribution(1)
        from_sibling(3)
        forward(3)
        hid_of(1).start()
        input_grad(3)
        got_all(2)
        contribution(3, fin_b)
        from_sibling(2)
        forward(2)
        input_grad(2)
        for k in order:
            leg(k).wait_recv()
            leg_on(k).start()
        contribution(2, m_of)
        for k in order:
            m_of(k).wait_recv()
            merge(po.at[1], k)
            fin_a(k, po.at[1]).start()
        weight_grads()
        hidden_out(1)
        totals()
        for k in range(K):
            odd_ring(k).wait_send()
            odd_up(k).wait_send()
            odd_opp(k).wait_send()
            fin_a(k, po.at[1]).wait_send()
            fin_b(k).wait_send()
            leg_on(k).wait_send()
        for copy in odd_cots:
            copy.wait_send()

    cot_opp.wait_send()
    for s in range(4):
        for k in range(K):
            sib_x(s, k).wait_send()
        sib_c(s).wait_send()
        sib_ps(s).wait_send()
    for k in range(K):
        m_of(k).wait_send()
    for j in range(2):
        hid_of(j).wait_send()


def store(*refs):
    count = len(refs) // 2
    sem = refs[-1]
    copies = [pltpu.make_async_copy(refs[i], refs[count + i], sem.at[i]) for i in range(count)]
    for copy in copies:
        copy.start()
    for copy in copies:
        copy.wait()


def per_device(experts, tokens, cotangent, gate_weights, tile_expert, w_gate, w_up):
    _, tile, width = tokens.shape
    quarter = w_gate.shape[2]
    groups = gate_weights.shape[0]
    half = 2 * quarter
    hbm = pl.BlockSpec(memory_space=pltpu.HBM)
    dma = pltpu.SemaphoreType.DMA
    vmem = pl.BlockSpec(memory_space=pltpu.VMEM)
    shapes = (tokens.shape, (groups, tile, quarter), w_gate.shape, w_up.shape)
    parts = pl.pallas_call(
        functools.partial(kernel, experts),
        out_shape=tuple(pltpu.VMEM(shape, BF16) for shape in shapes),
        in_specs=[hbm, hbm, hbm, pl.BlockSpec(memory_space=pltpu.SMEM), hbm, hbm],
        out_specs=(vmem, vmem, vmem, vmem),
        scratch_shapes=[
            pltpu.VMEM((4, 2 * tile, width), BF16),
            pltpu.VMEM((tile, width), BF16),
            pltpu.VMEM((4, tile, half), BF16),
            pltpu.VMEM((4, tile, quarter), BF16),
            pltpu.VMEM((2, groups, tile), F32),
            pltpu.VMEM((width, quarter), BF16),
            pltpu.VMEM((width, quarter), BF16),
            pltpu.VMEM((4, 2 * tile, half), BF16),
            pltpu.VMEM((4, 2 * tile, quarter), BF16),
            pltpu.VMEM((2, 2 * tile, quarter), BF16),
            pltpu.VMEM((4, tile, width), BF16),
            pltpu.VMEM((4, tile, width), BF16),
            pltpu.VMEM((4, tile, width), BF16),
            pltpu.VMEM((tile, width), BF16),
            pltpu.VMEM((tile, width), BF16),
            pltpu.VMEM((2, tile, width), BF16),
            pltpu.VMEM((tile, width), BF16),
            dma((2 * K,)), dma((K,)), dma((2 * K,)),
            dma((K,)), dma((K,)),
            dma((K,)),
            dma((4 * K,)), dma((4 * K,)),
            dma((5,)), dma((5,)), dma((4,)), dma((4,)),
            dma((4,)), dma((4,)),
            dma((K,)), dma((K,)),
            dma((K,)), dma((K,)),
            dma((2 * K,)), dma((2 * K,)),
            dma((K,)), dma((K,)),
            dma((2,)), dma((2,)),
            dma((4,)), dma((2,)),
        ],
        compiler_params=pltpu.CompilerParams(
            collective_id=0, has_side_effects=True, vmem_limit_bytes=62_192_000
        ),
    )(tokens, cotangent, gate_weights, tile_expert, w_gate, w_up)
    return pl.pallas_call(
        store,
        out_shape=tuple(jax.ShapeDtypeStruct(shape, BF16) for shape in shapes),
        in_specs=[pl.BlockSpec(memory_space=pl.ANY)] * 4,
        out_specs=(hbm, hbm, hbm, hbm),
        scratch_shapes=[dma((4,))],
        compiler_params=pltpu.CompilerParams(vmem_limit_bytes=1 << 20),
    )(*parts)


def solution(mesh):
    placed = (
        P("dp", "expert", None),
        P("dp", "expert", None),
        P(),
        P(),
        P("expert", None, "dp"),
        P("expert", None, "dp"),
    )
    return jax.shard_map(
        functools.partial(per_device, mesh.shape["expert"]),
        mesh=mesh,
        in_specs=placed,
        out_specs=(
            P("dp", "expert", None),
            P(None, "expert", "dp"),
            P("expert", None, "dp"),
            P("expert", None, "dp"),
        ),
        check_vma=False,
    )
```

```python
import functools

import jax
import jax.numpy as jnp
from jax import lax
from jax.experimental import pallas as pl
from jax.experimental.pallas import tpu as pltpu
from jax.sharding import PartitionSpec as P

MESH = pl.DeviceIdType.MESH
F32 = jnp.float32
BF16 = jnp.bfloat16
K = 4
N_COLS = 512


def dot_nn(a, b):
    return lax.dot_general(a, b, (((1,), (0,)), ((), ())), preferred_element_type=F32)


def dot_nt(a, b):
    return lax.dot_general(a, b, (((1,), (1,)), ((), ())), preferred_element_type=F32)


def dot_tn(a, b):
    return lax.dot_general(a, b, (((0,), (0,)), ((), ())), preferred_element_type=F32)


def kernel(
    experts,
    tok, cot, gw, te, wg_hbm, wu_hbm,
    dtok, hid, ggrad, ugrad,
    xr, xrelay, ch, cs, gwv, wg, wu, gu, hv, hb, po, ps, sp, mv, zc, fin, rl,
    s_ring, r_relay, r_x, s_opp, r_opp, s_z, s_sib, r_sib, s_cot, r_cot, s_sc, r_sc,
    s_ps, r_ps, s_m, r_m, s_zc, r_zc, s_fin, r_fin, s_leg, r_leg, s_hid, r_hid,
    l_in, l_gw,
):
    tile = tok.shape[1]
    width = tok.shape[2]
    quarter = wg_hbm.shape[2]
    half = 2 * quarter
    rows = tile // K
    d = lax.axis_index("dp")
    e = lax.axis_index("expert")
    hi, c = d // 2, d % 2
    lo = e % 2
    prev = (e + experts - 1) % experts

    y_e = e + 1 - 2 * lo
    yp = ((d + 2 * lo) % 4, y_e)
    ym = ((d + 2 * (1 - lo)) % 4, y_e)
    opp = ((d + 2) % 4, e)
    sib = (d + 1 - 2 * c, e)
    zn = (d, (e + 2) % experts)
    zp = (d, (e + experts - 2) % experts)
    nxt = (d, (e + 1) % experts)
    nx2 = ((d + 2) % 4, (e + 1) % experts)
    prv = (d, prev)
    pr2 = ((d + 2) % 4, prev)

    def remote(src, dst, send, recv, dev):
        return pltpu.make_async_remote_copy(
            src_ref=src, dst_ref=dst, send_sem=send, recv_sem=recv, device_id=dev, device_id_type=MESH
        )

    def arrived(dst, recv):
        remote(dst, dst, s_m.at[0], recv, sib).wait_recv()

    def sent(src, send):
        remote(src, src, send, r_m.at[0], sib).wait_send()

    def chunk(k, base=0, count=1):
        return pl.ds(base + k * rows, rows * count)

    even = lo == 0
    odd = lo == 1

    own_x = pltpu.make_async_copy(tok.at[0], xr.at[0, pl.ds(0, tile)], l_in.at[0])
    own_c = pltpu.make_async_copy(
        cot.at[0, :, pl.ds(pl.multiple_of(hi * half, half), half)], ch.at[0], l_in.at[1]
    )
    load_g = pltpu.make_async_copy(wg_hbm.at[0], wg, l_in.at[2])
    load_u = pltpu.make_async_copy(wu_hbm.at[0], wu, l_in.at[3])
    gw_own = pltpu.make_async_copy(gw.at[:, pl.ds(pl.multiple_of(e * tile, tile), tile)], gwv.at[0], l_gw.at[0])
    gw_prev = pltpu.make_async_copy(
        gw.at[:, pl.ds(pl.multiple_of(prev * tile, tile), tile)], gwv.at[1], l_gw.at[1]
    )
    own_x.start()
    own_c.start()
    load_g.start()
    load_u.start()
    gw_own.start()
    gw_prev.start()

    barrier = pltpu.get_barrier_semaphore()

    def greet(devices):
        for dev in devices:
            pl.semaphore_signal(barrier, inc=1, device_id=dev, device_id_type=MESH)
        pl.semaphore_wait(barrier, 7)

    mine = pl.ds(pl.multiple_of(c * quarter, quarter), quarter)
    other = pl.ds(pl.multiple_of((1 - c) * quarter, quarter), quarter)

    hk = K // 2
    pairs = [(i, K - 1 - i) for i in range(hk)]
    order = [k for pair in pairs for k in pair]
    low, high = pl.ds(0, tile // 2), pl.ds(tile // 2, tile // 2)

    def cot_to(h, r, slot, i, recv, dev):
        h = lax.rem(h, 2)
        return remote(
            cot.at[0, r, pl.ds(pl.multiple_of(h * half, half), half)],
            ch.at[slot, r], s_cot.at[i], r_cot.at[recv], dev,
        )

    all_rows = pl.ds(0, tile)
    cot_opp = cot_to(hi + 1, all_rows, 2, 4, 4, opp)

    def x_to(k, slot, i, dev):
        return remote(
            tok.at[0, chunk(k)], xr.at[slot, chunk(k)], s_ring.at[i], r_x.at[(0 if slot == 1 else K) + k], dev
        )

    def even_first(k):
        return x_to(k, 1, k, yp if k < hk else ym)

    def even_last(k):
        return x_to(k, 3, K + k, ym if k < hk else yp)

    even_cots = [
        cot_to(hi, low, 1, 0, 0, yp), cot_to(hi + 1, high, 1, 1, 1, ym),
        cot_to(hi + 1, low, 3, 2, 2, ym), cot_to(hi, high, 3, 3, 3, yp),
    ]

    def odd_ring(k):
        return remote(
            tok.at[0, chunk(k)], xrelay.at[chunk(k)], s_ring.at[k], r_relay.at[k], yp if k < hk else ym
        )

    def odd_up(k):
        return x_to(k, 3, K + k, nxt if k < hk else nx2)

    odd_cots = [
        cot_to(hi + 1, low, 1, 0, 0, nx2), cot_to(hi, high, 1, 1, 1, nxt),
        cot_to(hi, low, 3, 2, 2, nxt), cot_to(hi + 1, high, 3, 3, 3, nx2),
    ]

    @pl.when(even)
    def _():
        greet((yp, ym, sib, zn, zp, opp, prv, pr2))
        for k in order:
            even_first(k).start()

    @pl.when(odd)
    def _():
        greet((yp, ym, sib, opp, zn, nxt))
        for k in order:
            odd_up(k).start()
            odd_ring(k).start()

    def sib_x(s, k):
        return remote(
            xr.at[s, chunk(k)], xr.at[s, chunk(k, tile)], s_sib.at[K * s + k], r_sib.at[K * s + k], sib
        )

    def sib_c(s):
        return remote(ch.at[s, :, other], cs.at[s], s_sc.at[s], r_sc.at[s], sib)

    def from_sibling(s):
        for k in range(K):
            sib_x(s, k).wait_recv()
        sib_c(s).wait_recv()

    own_x.wait()
    own_c.wait()
    for k in range(K):
        sib_x(0, k).start()
    sib_c(0).start()

    eye = lax.broadcasted_iota(jnp.int32, (tile, tile), 0) == lax.broadcasted_iota(jnp.int32, (tile, tile), 1)
    first_lanes = lax.broadcasted_iota(jnp.int32, (1, tile), 1) < tile // 2
    gw_own.wait()
    gw_prev.wait()

    gh_one = (hi + 1 - lo) % 2
    gh_three = (hi + lo) % 2

    def weights_of(gh, core, place, which):
        group = gh * 2 + core
        routed = jnp.where(te[group, place] == e, jnp.float32(1.0), jnp.float32(0.0))
        return gwv[which, pl.ds(group, 1), :] * routed

    def scale_of(s, core):
        if s % 2 == 0:
            line = weights_of(hi if s == 0 else 1 - hi, core, e, 0)
        else:
            one = weights_of(gh_one, core, prev, 1)
            three = weights_of(gh_three, core, prev, 1)
            line = jnp.where(first_lanes, one, three) if s == 1 else jnp.where(first_lanes, three, one)
        spread = jnp.where(eye, jnp.broadcast_to(line, (tile, tile)), jnp.float32(0.0))
        return jnp.sum(spread, axis=1, keepdims=True)

    def forward(s):
        x = xr[s]
        gate = dot_nn(x, wg[...])
        up = dot_nn(x, wu[...])
        for part in range(2):
            w = scale_of(s, c if part == 0 else 1 - c)
            r = slice(part * tile, (part + 1) * tile)
            dh = (ch[s, :, mine] if part == 0 else cs[s]).astype(F32)
            g, u = gate[r], up[r]
            sg = jax.nn.sigmoid(g)
            act = g * sg
            hv[s, r, :] = ((w * act) * u).astype(BF16)
            ag = w * dh
            gu[s, r, 0:quarter] = (ag * u * sg * (1.0 + g * (1.0 - sg))).astype(BF16)
            gu[s, r, quarter:half] = (ag * act).astype(BF16)

    def sib_ps(s):
        return remote(ps.at[s], sp.at[s], s_ps.at[s], r_ps.at[s], sib)

    def input_grad(s):
        gg = gu[s, :, 0:quarter]
        ug = gu[s, :, quarter:half]

        @pl.loop(0, width // N_COLS)
        def _(n):
            cols = pl.ds(pl.multiple_of(n * N_COLS, N_COLS), N_COLS)
            part = dot_nt(gg, wg[cols, :]) + dot_nt(ug, wu[cols, :])
            po[s, :, cols] = part[0:tile].astype(BF16)
            ps[s, :, cols] = part[tile:].astype(BF16)

        sib_ps(s).start()

    def contribution(s, send=None):
        sib_ps(s).wait_recv()
        for k in order:
            r = chunk(k)
            po[s, r, :] = (po[s, r, :].astype(F32) + sp[s, r, :].astype(F32)).astype(BF16)
            if send is not None:
                send(k).start()

    def relay_z(k):
        return remote(xrelay.at[chunk(k)], xr.at[1, chunk(k)], s_z.at[k], r_x.at[k], zn)

    def relay_opp(k, src):
        return remote(src, xr.at[2, chunk(k)], s_opp.at[k], r_opp.at[k], yp if k < hk else ym)

    def even_opp(k):
        return relay_opp(k, xrelay.at[chunk(k)])

    def odd_opp(k):
        return relay_opp(k, xr.at[1, chunk(k)])

    def got_relay(k):
        arrived(xrelay.at[chunk(k)], r_relay.at[k])

    def got_cot(s):
        if s == 2:
            arrived(ch.at[2], r_cot.at[4])
        else:
            arrived(ch.at[s, low], r_cot.at[s - 1])
            arrived(ch.at[s, high], r_cot.at[s])
        sib_c(s).start()

    def got(s, k):
        arrived(xr.at[s, chunk(k)], r_opp.at[k] if s == 2 else r_x.at[(0 if s == 1 else K) + k])
        sib_x(s, k).start()

    def got_all(s):
        got_cot(s)
        for k in order:
            got(s, k)

    def m_of(k):
        return remote(po.at[2, chunk(k)], mv.at[chunk(k)], s_m.at[k], r_m.at[k], ym if k < hk else yp)

    def fin_a(k, src):
        j = 0 if k < hk else 1
        return remote(
            src.at[chunk(k)], fin.at[j, chunk(k)], s_fin.at[k], r_fin.at[K * j + k], ym if k < hk else yp
        )

    def fin_b(k):
        j = 1 if k < hk else 0
        return remote(
            po.at[3, chunk(k)], fin.at[j, chunk(k)], s_fin.at[K + k], r_fin.at[K * j + k], yp if k < hk else ym
        )

    def zq(k):
        return remote(po.at[1, chunk(k)], zc.at[chunk(k)], s_zc.at[k], r_zc.at[k], zp)

    def leg(k):
        return remote(po.at[3, chunk(k)], rl.at[chunk(k)], s_leg.at[k], r_leg.at[k], yp if k < hk else ym)

    def leg_on(k):
        j = 1 if k < hk else 0
        return remote(rl.at[chunk(k)], fin.at[j, chunk(k)], s_leg.at[k], r_fin.at[K * j + k], zp)

    def hid_of(j):
        return remote(hv.at[1 + 2 * j], hb.at[j], s_hid.at[j], r_hid.at[j], prv)

    def merge(dst, k):
        r = chunk(k)
        dst[r, :] = (dst[r, :].astype(F32) + mv[r, :].astype(F32)).astype(BF16)

    def weight_grads():
        @pl.loop(0, width // N_COLS)
        def _(n):
            cols = pl.ds(pl.multiple_of(n * N_COLS, N_COLS), N_COLS)
            x = xr[:, :, cols].reshape(8 * tile, N_COLS)
            grads = gu[...].reshape(8 * tile, half)
            total = dot_tn(x, grads) * (1.0 / tile)
            ggrad[0, cols, :] = total[:, 0:quarter].astype(BF16)
            ugrad[0, cols, :] = total[:, quarter:].astype(BF16)

    def hidden_out(first):
        for j in range(2):
            hid_of(j).wait_recv()
        for slot in (0, 2):
            gh = hi if slot == 0 else 1 - hi
            lead = first if slot == 0 else 1 - first
            for part in range(2):
                group = gh * 2 + (c if part == 0 else 1 - c)
                for i in range(2):
                    r = slice(part * tile + i * (tile // 2), part * tile + (i + 1) * (tile // 2))
                    back = hb[lead if i == 0 else 1 - lead, r, :]
                    hid[group, i * (tile // 2) : (i + 1) * (tile // 2), :] = (
                        hv[slot, r, :].astype(F32) + back.astype(F32)
                    ).astype(BF16)

    def totals():
        for k in order:
            for j in range(2):
                arrived(fin.at[j, chunk(k)], r_fin.at[K * j + k])
            r = chunk(k)
            dtok[0, r, :] = (po[0, r, :].astype(F32) + fin[0, r, :].astype(F32) + fin[1, r, :].astype(F32)).astype(
                BF16
            )

    load_g.wait()
    load_u.wait()

    @pl.when(even)
    def _():
        for k in [k for i in range(hk) for k in (hk + i, hk - 1 - i)]:
            even_last(k).start()
        for copy in even_cots[2:]:
            copy.start()
        for copy in even_cots[:2]:
            copy.start()
        cot_opp.start()
        from_sibling(0)
        forward(0)
        for k in order[:hk]:
            got_relay(k)
            relay_z(k).start()
            even_opp(k).start()
        input_grad(0)
        for k in order[hk:]:
            got_relay(k)
            relay_z(k).start()
            even_opp(k).start()
        contribution(0)
        got_all(3)
        from_sibling(3)
        forward(3)
        hid_of(1).start()
        input_grad(3)
        got_all(1)
        contribution(3, leg)
        from_sibling(1)
        forward(1)
        hid_of(0).start()
        input_grad(1)
        got_all(2)
        contribution(1, zq)
        from_sibling(2)
        forward(2)
        input_grad(2)
        contribution(2, m_of)
        for k in order:
            m_of(k).wait_recv()
            zq(k).wait_recv()
            merge(zc, k)
            fin_a(k, zc).start()
        weight_grads()
        hidden_out(0)
        totals()
        for k in range(K):
            even_first(k).wait_send()
            even_last(k).wait_send()
            relay_z(k).wait_send()
            even_opp(k).wait_send()
            zq(k).wait_send()
            leg(k).wait_send()
            fin_a(k, zc).wait_send()
        for copy in even_cots:
            copy.wait_send()

    @pl.when(odd)
    def _():
        for copy in odd_cots[2:]:
            copy.start()
        for copy in odd_cots[:2]:
            copy.start()
        cot_opp.start()
        from_sibling(0)
        forward(0)
        for k in order[:hk]:
            got(1, k)
            odd_opp(k).start()
        input_grad(0)
        for k in order[hk:]:
            got(1, k)
            odd_opp(k).start()
        got_cot(1)
        contribution(0)
        from_sibling(1)
        forward(1)
        hid_of(0).start()
        input_grad(1)
        got_all(3)
        contribution(1)
        from_sibling(3)
        forward(3)
        hid_of(1).start()
        input_grad(3)
        got_all(2)
        contribution(3, fin_b)
        from_sibling(2)
        forward(2)
        input_grad(2)
        for k in order:
            leg(k).wait_recv()
            leg_on(k).start()
        contribution(2, m_of)
        for k in order:
            m_of(k).wait_recv()
            merge(po.at[1], k)
            fin_a(k, po.at[1]).start()
        weight_grads()
        hidden_out(1)
        totals()
        for k in range(K):
            odd_ring(k).wait_send()
            odd_up(k).wait_send()
            odd_opp(k).wait_send()
            fin_a(k, po.at[1]).wait_send()
            fin_b(k).wait_send()
            leg_on(k).wait_send()
        for copy in odd_cots:
            copy.wait_send()

    cot_opp.wait_send()
    for s in range(4):
        for k in range(K):
            sib_x(s, k).wait_send()
        sib_c(s).wait_send()
        sib_ps(s).wait_send()
    for k in range(K):
        m_of(k).wait_send()
    for j in range(2):
        hid_of(j).wait_send()


def store(*refs):
    count = len(refs) // 2
    sem = refs[-1]
    copies = [pltpu.make_async_copy(refs[i], refs[count + i], sem.at[i]) for i in range(count)]
    for copy in copies:
        copy.start()
    for copy in copies:
        copy.wait()


def per_device(experts, tokens, cotangent, gate_weights, tile_expert, w_gate, w_up):
    _, tile, width = tokens.shape
    quarter = w_gate.shape[2]
    groups = gate_weights.shape[0]
    half = 2 * quarter
    hbm = pl.BlockSpec(memory_space=pltpu.HBM)
    dma = pltpu.SemaphoreType.DMA
    vmem = pl.BlockSpec(memory_space=pltpu.VMEM)
    shapes = (tokens.shape, (groups, tile, quarter), w_gate.shape, w_up.shape)
    parts = pl.pallas_call(
        functools.partial(kernel, experts),
        out_shape=tuple(pltpu.VMEM(shape, BF16) for shape in shapes),
        in_specs=[hbm, hbm, hbm, pl.BlockSpec(memory_space=pltpu.SMEM), hbm, hbm],
        out_specs=(vmem, vmem, vmem, vmem),
        scratch_shapes=[
            pltpu.VMEM((4, 2 * tile, width), BF16),
            pltpu.VMEM((tile, width), BF16),
            pltpu.VMEM((4, tile, half), BF16),
            pltpu.VMEM((4, tile, quarter), BF16),
            pltpu.VMEM((2, groups, tile), F32),
            pltpu.VMEM((width, quarter), BF16),
            pltpu.VMEM((width, quarter), BF16),
            pltpu.VMEM((4, 2 * tile, half), BF16),
            pltpu.VMEM((4, 2 * tile, quarter), BF16),
            pltpu.VMEM((2, 2 * tile, quarter), BF16),
            pltpu.VMEM((4, tile, width), BF16),
            pltpu.VMEM((4, tile, width), BF16),
            pltpu.VMEM((4, tile, width), BF16),
            pltpu.VMEM((tile, width), BF16),
            pltpu.VMEM((tile, width), BF16),
            pltpu.VMEM((2, tile, width), BF16),
            pltpu.VMEM((tile, width), BF16),
            dma((2 * K,)), dma((K,)), dma((2 * K,)),
            dma((K,)), dma((K,)),
            dma((K,)),
            dma((4 * K,)), dma((4 * K,)),
            dma((5,)), dma((5,)), dma((4,)), dma((4,)),
            dma((4,)), dma((4,)),
            dma((K,)), dma((K,)),
            dma((K,)), dma((K,)),
            dma((2 * K,)), dma((2 * K,)),
            dma((K,)), dma((K,)),
            dma((2,)), dma((2,)),
            dma((4,)), dma((2,)),
        ],
        compiler_params=pltpu.CompilerParams(
            collective_id=0, has_side_effects=True, vmem_limit_bytes=62_192_000
        ),
    )(tokens, cotangent, gate_weights, tile_expert, w_gate, w_up)
    return pl.pallas_call(
        store,
        out_shape=tuple(jax.ShapeDtypeStruct(shape, BF16) for shape in shapes),
        in_specs=[pl.BlockSpec(memory_space=pl.ANY)] * 4,
        out_specs=(hbm, hbm, hbm, hbm),
        scratch_shapes=[dma((4,))],
        compiler_params=pltpu.CompilerParams(vmem_limit_bytes=1 << 20),
    )(*parts)


def solution(mesh):
    placed = (
        P("dp", "expert", None),
        P("dp", "expert", None),
        P(),
        P(),
        P("expert", None, "dp"),
        P("expert", None, "dp"),
    )
    return jax.shard_map(
        functools.partial(per_device, mesh.shape["expert"]),
        mesh=mesh,
        in_specs=placed,
        out_specs=(
            P("dp", "expert", None),
            P(None, "expert", "dp"),
            P("expert", None, "dp"),
            P("expert", None, "dp"),
        ),
        check_vma=False,
    )
```

```python
import functools

import jax
import jax.numpy as jnp
from jax import lax
from jax.experimental import pallas as pl
from jax.experimental.pallas import tpu as pltpu
from jax.sharding import PartitionSpec as P

MESH = pl.DeviceIdType.MESH
F32 = jnp.float32
BF16 = jnp.bfloat16
K = 4
N_COLS = 896


def dot_nn(a, b):
    return lax.dot_general(a, b, (((1,), (0,)), ((), ())), preferred_element_type=F32)


def dot_nt(a, b):
    return lax.dot_general(a, b, (((1,), (1,)), ((), ())), preferred_element_type=F32)


def dot_tn(a, b):
    return lax.dot_general(a, b, (((0,), (0,)), ((), ())), preferred_element_type=F32)


def kernel(
    experts,
    tok, cot, gw, te, wg_hbm, wu_hbm,
    dtok, hid, ggrad, ugrad,
    xr, xrelay, ch, cs, gwv, wg, wu, gu, hv, hb, po, ps, sp, mv, zc, fin, rl,
    s_ring, r_relay, r_x, s_opp, r_opp, s_z, s_sib, r_sib, s_cot, r_cot, s_sc, r_sc,
    s_ps, r_ps, s_m, r_m, s_zc, r_zc, s_fin, r_fin, s_leg, r_leg, s_hid, r_hid,
    l_in, l_gw,
):
    tile = tok.shape[1]
    width = tok.shape[2]
    quarter = wg_hbm.shape[2]
    half = 2 * quarter
    rows = tile // K
    d = lax.axis_index("dp")
    e = lax.axis_index("expert")
    hi, c = d // 2, d % 2
    lo = e % 2
    prev = (e + experts - 1) % experts

    y_e = e + 1 - 2 * lo
    yp = ((d + 2 * lo) % 4, y_e)
    ym = ((d + 2 * (1 - lo)) % 4, y_e)
    opp = ((d + 2) % 4, e)
    sib = (d + 1 - 2 * c, e)
    zn = (d, (e + 2) % experts)
    zp = (d, (e + experts - 2) % experts)
    nxt = (d, (e + 1) % experts)
    nx2 = ((d + 2) % 4, (e + 1) % experts)
    prv = (d, prev)
    pr2 = ((d + 2) % 4, prev)

    def remote(src, dst, send, recv, dev):
        return pltpu.make_async_remote_copy(
            src_ref=src, dst_ref=dst, send_sem=send, recv_sem=recv, device_id=dev, device_id_type=MESH
        )

    def arrived(dst, recv):
        remote(dst, dst, s_m.at[0], recv, sib).wait_recv()

    def sent(src, send):
        remote(src, src, send, r_m.at[0], sib).wait_send()

    def chunk(k, base=0, count=1):
        return pl.ds(base + k * rows, rows * count)

    even = lo == 0
    odd = lo == 1

    own_x = pltpu.make_async_copy(tok.at[0], xr.at[0, pl.ds(0, tile)], l_in.at[0])
    own_c = pltpu.make_async_copy(
        cot.at[0, :, pl.ds(pl.multiple_of(hi * half, half), half)], ch.at[0], l_in.at[1]
    )
    load_g = pltpu.make_async_copy(wg_hbm.at[0], wg, l_in.at[2])
    load_u = pltpu.make_async_copy(wu_hbm.at[0], wu, l_in.at[3])
    gw_own = pltpu.make_async_copy(gw.at[:, pl.ds(pl.multiple_of(e * tile, tile), tile)], gwv.at[0], l_gw.at[0])
    gw_prev = pltpu.make_async_copy(
        gw.at[:, pl.ds(pl.multiple_of(prev * tile, tile), tile)], gwv.at[1], l_gw.at[1]
    )
    own_x.start()
    own_c.start()
    load_g.start()
    load_u.start()
    gw_own.start()
    gw_prev.start()

    barrier = pltpu.get_barrier_semaphore()

    def greet(devices):
        for dev in devices:
            pl.semaphore_signal(barrier, inc=1, device_id=dev, device_id_type=MESH)
        pl.semaphore_wait(barrier, 7)

    mine = pl.ds(pl.multiple_of(c * quarter, quarter), quarter)
    other = pl.ds(pl.multiple_of((1 - c) * quarter, quarter), quarter)

    hk = K // 2
    pairs = [(i, K - 1 - i) for i in range(hk)]
    order = [k for pair in pairs for k in pair]
    low, high = pl.ds(0, tile // 2), pl.ds(tile // 2, tile // 2)

    def cot_to(h, r, slot, i, recv, dev):
        h = lax.rem(h, 2)
        return remote(
            cot.at[0, r, pl.ds(pl.multiple_of(h * half, half), half)],
            ch.at[slot, r], s_cot.at[i], r_cot.at[recv], dev,
        )

    all_rows = pl.ds(0, tile)
    cot_opp = cot_to(hi + 1, all_rows, 2, 4, 4, opp)

    def x_to(k, slot, i, dev):
        return remote(
            tok.at[0, chunk(k)], xr.at[slot, chunk(k)], s_ring.at[i], r_x.at[(0 if slot == 1 else K) + k], dev
        )

    def even_first(k):
        return x_to(k, 1, k, yp if k < hk else ym)

    def even_last(k):
        return x_to(k, 3, K + k, ym if k < hk else yp)

    even_cots = [
        cot_to(hi, low, 1, 0, 0, yp), cot_to(hi + 1, high, 1, 1, 1, ym),
        cot_to(hi + 1, low, 3, 2, 2, ym), cot_to(hi, high, 3, 3, 3, yp),
    ]

    def odd_ring(k):
        return remote(
            tok.at[0, chunk(k)], xrelay.at[chunk(k)], s_ring.at[k], r_relay.at[k], yp if k < hk else ym
        )

    def odd_up(k):
        return x_to(k, 3, K + k, nxt if k < hk else nx2)

    odd_cots = [
        cot_to(hi + 1, low, 1, 0, 0, nx2), cot_to(hi, high, 1, 1, 1, nxt),
        cot_to(hi, low, 3, 2, 2, nxt), cot_to(hi + 1, high, 3, 3, 3, nx2),
    ]

    @pl.when(even)
    def _():
        greet((yp, ym, sib, zn, zp, opp, prv, pr2))
        for k in order:
            even_first(k).start()

    @pl.when(odd)
    def _():
        greet((yp, ym, sib, opp, zn, nxt))
        for k in order:
            odd_up(k).start()
            odd_ring(k).start()

    def sib_x(s, k):
        return remote(
            xr.at[s, chunk(k)], xr.at[s, chunk(k, tile)], s_sib.at[K * s + k], r_sib.at[K * s + k], sib
        )

    def sib_c(s):
        return remote(ch.at[s, :, other], cs.at[s], s_sc.at[s], r_sc.at[s], sib)

    def from_sibling(s):
        for k in range(K):
            sib_x(s, k).wait_recv()
        sib_c(s).wait_recv()

    own_x.wait()
    own_c.wait()
    for k in range(K):
        sib_x(0, k).start()
    sib_c(0).start()

    eye = lax.broadcasted_iota(jnp.int32, (tile, tile), 0) == lax.broadcasted_iota(jnp.int32, (tile, tile), 1)
    first_lanes = lax.broadcasted_iota(jnp.int32, (1, tile), 1) < tile // 2
    gw_own.wait()
    gw_prev.wait()

    gh_one = (hi + 1 - lo) % 2
    gh_three = (hi + lo) % 2

    def weights_of(gh, core, place, which):
        group = gh * 2 + core
        routed = jnp.where(te[group, place] == e, jnp.float32(1.0), jnp.float32(0.0))
        return gwv[which, pl.ds(group, 1), :] * routed

    def scale_of(s, core):
        if s % 2 == 0:
            line = weights_of(hi if s == 0 else 1 - hi, core, e, 0)
        else:
            one = weights_of(gh_one, core, prev, 1)
            three = weights_of(gh_three, core, prev, 1)
            line = jnp.where(first_lanes, one, three) if s == 1 else jnp.where(first_lanes, three, one)
        spread = jnp.where(eye, jnp.broadcast_to(line, (tile, tile)), jnp.float32(0.0))
        return jnp.sum(spread, axis=1, keepdims=True)

    def forward(s):
        x = xr[s]
        gate = dot_nn(x, wg[...])
        up = dot_nn(x, wu[...])
        for part in range(2):
            w = scale_of(s, c if part == 0 else 1 - c)
            r = slice(part * tile, (part + 1) * tile)
            dh = (ch[s, :, mine] if part == 0 else cs[s]).astype(F32)
            g, u = gate[r], up[r]
            sg = jax.nn.sigmoid(g)
            act = g * sg
            hv[s, r, :] = ((w * act) * u).astype(BF16)
            ag = w * dh
            gu[s, r, 0:quarter] = (ag * u * sg * (1.0 + g * (1.0 - sg))).astype(BF16)
            gu[s, r, quarter:half] = (ag * act).astype(BF16)

    def sib_ps(s):
        return remote(ps.at[s], sp.at[s], s_ps.at[s], r_ps.at[s], sib)

    def input_grad(s):
        gg = gu[s, :, 0:quarter]
        ug = gu[s, :, quarter:half]

        @pl.loop(0, width // N_COLS)
        def _(n):
            cols = pl.ds(pl.multiple_of(n * N_COLS, N_COLS), N_COLS)
            part = dot_nt(gg, wg[cols, :]) + dot_nt(ug, wu[cols, :])
            po[s, :, cols] = part[0:tile].astype(BF16)
            ps[s, :, cols] = part[tile:].astype(BF16)

        sib_ps(s).start()

    def contribution(s, send=None):
        sib_ps(s).wait_recv()
        for k in order:
            r = chunk(k)
            po[s, r, :] = (po[s, r, :].astype(F32) + sp[s, r, :].astype(F32)).astype(BF16)
            if send is not None:
                send(k).start()

    def relay_z(k):
        return remote(xrelay.at[chunk(k)], xr.at[1, chunk(k)], s_z.at[k], r_x.at[k], zn)

    def relay_opp(k, src):
        return remote(src, xr.at[2, chunk(k)], s_opp.at[k], r_opp.at[k], yp if k < hk else ym)

    def even_opp(k):
        return relay_opp(k, xrelay.at[chunk(k)])

    def odd_opp(k):
        return relay_opp(k, xr.at[1, chunk(k)])

    def got_relay(k):
        arrived(xrelay.at[chunk(k)], r_relay.at[k])

    def got_cot(s):
        if s == 2:
            arrived(ch.at[2], r_cot.at[4])
        else:
            arrived(ch.at[s, low], r_cot.at[s - 1])
            arrived(ch.at[s, high], r_cot.at[s])
        sib_c(s).start()

    def got(s, k):
        arrived(xr.at[s, chunk(k)], r_opp.at[k] if s == 2 else r_x.at[(0 if s == 1 else K) + k])
        sib_x(s, k).start()

    def got_all(s):
        got_cot(s)
        for k in order:
            got(s, k)

    def m_of(k):
        return remote(po.at[2, chunk(k)], mv.at[chunk(k)], s_m.at[k], r_m.at[k], ym if k < hk else yp)

    def fin_a(k, src):
        j = 0 if k < hk else 1
        return remote(
            src.at[chunk(k)], fin.at[j, chunk(k)], s_fin.at[k], r_fin.at[K * j + k], ym if k < hk else yp
        )

    def fin_b(k):
        j = 1 if k < hk else 0
        return remote(
            po.at[3, chunk(k)], fin.at[j, chunk(k)], s_fin.at[K + k], r_fin.at[K * j + k], yp if k < hk else ym
        )

    def zq(k):
        return remote(po.at[1, chunk(k)], zc.at[chunk(k)], s_zc.at[k], r_zc.at[k], zp)

    def leg(k):
        return remote(po.at[3, chunk(k)], rl.at[chunk(k)], s_leg.at[k], r_leg.at[k], yp if k < hk else ym)

    def leg_on(k):
        j = 1 if k < hk else 0
        return remote(rl.at[chunk(k)], fin.at[j, chunk(k)], s_leg.at[k], r_fin.at[K * j + k], zp)

    def hid_of(j):
        return remote(hv.at[1 + 2 * j], hb.at[j], s_hid.at[j], r_hid.at[j], prv)

    def merge(dst, k):
        r = chunk(k)
        dst[r, :] = (dst[r, :].astype(F32) + mv[r, :].astype(F32)).astype(BF16)

    def weight_grads():
        @pl.loop(0, width // N_COLS)
        def _(n):
            cols = pl.ds(pl.multiple_of(n * N_COLS, N_COLS), N_COLS)
            x = xr[:, :, cols].reshape(8 * tile, N_COLS)
            grads = gu[...].reshape(8 * tile, half)
            total = dot_tn(x, grads) * (1.0 / tile)
            ggrad[0, cols, :] = total[:, 0:quarter].astype(BF16)
            ugrad[0, cols, :] = total[:, quarter:].astype(BF16)

    def hidden_out(first):
        for j in range(2):
            hid_of(j).wait_recv()
        for slot in (0, 2):
            gh = hi if slot == 0 else 1 - hi
            lead = first if slot == 0 else 1 - first
            for part in range(2):
                group = gh * 2 + (c if part == 0 else 1 - c)
                for i in range(2):
                    r = slice(part * tile + i * (tile // 2), part * tile + (i + 1) * (tile // 2))
                    back = hb[lead if i == 0 else 1 - lead, r, :]
                    hid[group, i * (tile // 2) : (i + 1) * (tile // 2), :] = (
                        hv[slot, r, :].astype(F32) + back.astype(F32)
                    ).astype(BF16)

    def totals():
        for k in order:
            for j in range(2):
                arrived(fin.at[j, chunk(k)], r_fin.at[K * j + k])
            r = chunk(k)
            dtok[0, r, :] = (po[0, r, :].astype(F32) + fin[0, r, :].astype(F32) + fin[1, r, :].astype(F32)).astype(
                BF16
            )

    load_g.wait()
    load_u.wait()

    @pl.when(even)
    def _():
        for k in [k for i in range(hk) for k in (hk + i, hk - 1 - i)]:
            even_last(k).start()
        for copy in even_cots[2:]:
            copy.start()
        for copy in even_cots[:2]:
            copy.start()
        cot_opp.start()
        from_sibling(0)
        forward(0)
        for k in order[:hk]:
            got_relay(k)
            relay_z(k).start()
            even_opp(k).start()
        input_grad(0)
        for k in order[hk:]:
            got_relay(k)
            relay_z(k).start()
            even_opp(k).start()
        contribution(0)
        got_all(3)
        from_sibling(3)
        forward(3)
        hid_of(1).start()
        input_grad(3)
        got_all(1)
        contribution(3, leg)
        from_sibling(1)
        forward(1)
        hid_of(0).start()
        input_grad(1)
        got_all(2)
        contribution(1, zq)
        from_sibling(2)
        forward(2)
        input_grad(2)
        contribution(2, m_of)
        for k in order:
            m_of(k).wait_recv()
            zq(k).wait_recv()
            merge(zc, k)
            fin_a(k, zc).start()
        weight_grads()
        hidden_out(0)
        totals()
        for k in range(K):
            even_first(k).wait_send()
            even_last(k).wait_send()
            relay_z(k).wait_send()
            even_opp(k).wait_send()
            zq(k).wait_send()
            leg(k).wait_send()
            fin_a(k, zc).wait_send()
        for copy in even_cots:
            copy.wait_send()

    @pl.when(odd)
    def _():
        for copy in odd_cots[2:]:
            copy.start()
        for copy in odd_cots[:2]:
            copy.start()
        cot_opp.start()
        from_sibling(0)
        forward(0)
        for k in order[:hk]:
            got(1, k)
            odd_opp(k).start()
        input_grad(0)
        for k in order[hk:]:
            got(1, k)
            odd_opp(k).start()
        got_cot(1)
        contribution(0)
        from_sibling(1)
        forward(1)
        hid_of(0).start()
        input_grad(1)
        got_all(3)
        contribution(1)
        from_sibling(3)
        forward(3)
        hid_of(1).start()
        input_grad(3)
        got_all(2)
        contribution(3, fin_b)
        from_sibling(2)
        forward(2)
        input_grad(2)
        for k in order:
            leg(k).wait_recv()
            leg_on(k).start()
        contribution(2, m_of)
        for k in order:
            m_of(k).wait_recv()
            merge(po.at[1], k)
            fin_a(k, po.at[1]).start()
        weight_grads()
        hidden_out(1)
        totals()
        for k in range(K):
            odd_ring(k).wait_send()
            odd_up(k).wait_send()
            odd_opp(k).wait_send()
            fin_a(k, po.at[1]).wait_send()
            fin_b(k).wait_send()
            leg_on(k).wait_send()
        for copy in odd_cots:
            copy.wait_send()

    cot_opp.wait_send()
    for s in range(4):
        for k in range(K):
            sib_x(s, k).wait_send()
        sib_c(s).wait_send()
        sib_ps(s).wait_send()
    for k in range(K):
        m_of(k).wait_send()
    for j in range(2):
        hid_of(j).wait_send()


def store(*refs):
    count = len(refs) // 2
    sem = refs[-1]
    copies = [pltpu.make_async_copy(refs[i], refs[count + i], sem.at[i]) for i in range(count)]
    for copy in copies:
        copy.start()
    for copy in copies:
        copy.wait()


def per_device(experts, tokens, cotangent, gate_weights, tile_expert, w_gate, w_up):
    _, tile, width = tokens.shape
    quarter = w_gate.shape[2]
    groups = gate_weights.shape[0]
    half = 2 * quarter
    hbm = pl.BlockSpec(memory_space=pltpu.HBM)
    dma = pltpu.SemaphoreType.DMA
    vmem = pl.BlockSpec(memory_space=pltpu.VMEM)
    shapes = (tokens.shape, (groups, tile, quarter), w_gate.shape, w_up.shape)
    parts = pl.pallas_call(
        functools.partial(kernel, experts),
        out_shape=tuple(pltpu.VMEM(shape, BF16) for shape in shapes),
        in_specs=[hbm, hbm, hbm, pl.BlockSpec(memory_space=pltpu.SMEM), hbm, hbm],
        out_specs=(vmem, vmem, vmem, vmem),
        scratch_shapes=[
            pltpu.VMEM((4, 2 * tile, width), BF16),
            pltpu.VMEM((tile, width), BF16),
            pltpu.VMEM((4, tile, half), BF16),
            pltpu.VMEM((4, tile, quarter), BF16),
            pltpu.VMEM((2, groups, tile), F32),
            pltpu.VMEM((width, quarter), BF16),
            pltpu.VMEM((width, quarter), BF16),
            pltpu.VMEM((4, 2 * tile, half), BF16),
            pltpu.VMEM((4, 2 * tile, quarter), BF16),
            pltpu.VMEM((2, 2 * tile, quarter), BF16),
            pltpu.VMEM((4, tile, width), BF16),
            pltpu.VMEM((4, tile, width), BF16),
            pltpu.VMEM((4, tile, width), BF16),
            pltpu.VMEM((tile, width), BF16),
            pltpu.VMEM((tile, width), BF16),
            pltpu.VMEM((2, tile, width), BF16),
            pltpu.VMEM((tile, width), BF16),
            dma((2 * K,)), dma((K,)), dma((2 * K,)),
            dma((K,)), dma((K,)),
            dma((K,)),
            dma((4 * K,)), dma((4 * K,)),
            dma((5,)), dma((5,)), dma((4,)), dma((4,)),
            dma((4,)), dma((4,)),
            dma((K,)), dma((K,)),
            dma((K,)), dma((K,)),
            dma((2 * K,)), dma((2 * K,)),
            dma((K,)), dma((K,)),
            dma((2,)), dma((2,)),
            dma((4,)), dma((2,)),
        ],
        compiler_params=pltpu.CompilerParams(
            collective_id=0, has_side_effects=True, vmem_limit_bytes=62_192_000
        ),
    )(tokens, cotangent, gate_weights, tile_expert, w_gate, w_up)
    return pl.pallas_call(
        store,
        out_shape=tuple(jax.ShapeDtypeStruct(shape, BF16) for shape in shapes),
        in_specs=[pl.BlockSpec(memory_space=pl.ANY)] * 4,
        out_specs=(hbm, hbm, hbm, hbm),
        scratch_shapes=[dma((4,))],
        compiler_params=pltpu.CompilerParams(vmem_limit_bytes=1 << 20),
    )(*parts)


def solution(mesh):
    placed = (
        P("dp", "expert", None),
        P("dp", "expert", None),
        P(),
        P(),
        P("expert", None, "dp"),
        P("expert", None, "dp"),
    )
    return jax.shard_map(
        functools.partial(per_device, mesh.shape["expert"]),
        mesh=mesh,
        in_specs=placed,
        out_specs=(
            P("dp", "expert", None),
            P(None, "expert", "dp"),
            P("expert", None, "dp"),
            P("expert", None, "dp"),
        ),
        check_vma=False,
    )
```
